32 devices in a mesh: dp: 8 (over y, x, core), tensor: 4 (over z).
Axes of the slice: x: 2, y: 2, z: 4, core: 2. Of those that a mesh axis runs over, the one named last changes fastest.
Arguments:
- residual_in: bfloat16 [8192, 1024], P(('dp', 'tensor')), may hold values from -16 to 16
- segments: int32 [8192], P('dp'), may hold values from -1 to 16, as said below
- positions: int32 [8192], P('dp'), may hold values from 0 to 799, as said below
- query_weight: bfloat16 [1024, 1024], P('dp', 'tensor'), may hold values from -0.1875 to 0.1875
- key_weight: bfloat16 [1024, 1024], P('dp', 'tensor'), may hold values from -0.1875 to 0.1875
- value_weight: bfloat16 [1024, 1024], P('dp', 'tensor'), may hold values from -0.1875 to 0.1875
- out_weight: bfloat16 [1024, 1024], P('dp', 'tensor'), may hold values from -0.75 to 0.75
- up_weight: bfloat16 [1024, 4096], P('dp', 'tensor'), may hold values from -0.1875 to 0.1875
- down_weight: bfloat16 [1024, 4096], P('dp', 'tensor'), may hold values from -0.09375 to 0.09375
- norm_gains: float32 [4, 1024], P(None, ('dp', 'tensor')), may hold values from 0.25 to 1.75
- norm_biases: float32 [4, 1024], P(None, ('dp', 'tensor')), may hold values from -1 to 1
- cotangent: bfloat16 [8192, 1024], P(('dp', 'tensor')), may hold values from -6 to 6
Outputs:
- layer_out: bfloat16 [8192, 1024], P(('dp', 'tensor'))
- grad_input: bfloat16 [8192, 1024], P(('dp', 'tensor'))
- grad_query_weight: float32 [1024, 1024], P('dp', 'tensor')
- grad_key_weight: float32 [1024, 1024], P('dp', 'tensor')
- grad_value_weight: float32 [1024, 1024], P('dp', 'tensor')
- grad_out_weight: float32 [1024, 1024], P('dp', 'tensor')
- grad_up_weight: float32 [1024, 4096], P('dp', 'tensor')
- grad_down_weight: float32 [1024, 4096], P('dp', 'tensor')
- grad_norm_gains: float32 [4, 1024], P(None, ('dp', 'tensor'))
- grad_norm_biases: float32 [4, 1024], P(None, ('dp', 'tensor'))
- rms_stats: float32 [3], replicated
The draws below stay inside these ranges and needn't reach their ends.
Inputs may be any that keep to these rules, and one draw needn't show every extreme that they name: `segments`: each sequence of 1024 tokens holds whole documents of 60 to 800 tokens, numbered 0, 1, 2 in order, and then padding with -1; the first document of some sequence has exactly 800 tokens, and some other sequence holds 17 documents of 60 tokens. `positions`: the position of a token within its document, counted from 0; 0 on padding.
All inputs are finite; a program needn't handle non-finite values.
Results may differ from the reference program's by a relative error of at most 0.015.
Values may be sent and summed in bfloat16 or wider, within the bound.
No kernel may reach another device: no remote copies, remote signals or barrier semaphores. Data moves between devices by JAX's collectives and lax.ppermute only.
A program may use at most 128 MiB of HBM per device.

```python
import math
import jax
import jax.numpy as jnp
from jax import lax

D = 1024
HEAD_DIM = 64
FF = 4096
SEQ_LEN = 1024
DOC_MIN = 60
DOC_MAX = 800
TOKENS = 8192
N_DP = 8


def draw_residual_in(key, part):
    row_frac = jnp.arange(TOKENS, dtype=jnp.float32)[:, None] / max(TOKENS - 1, 1)
    values = jnp.clip(jax.random.normal(key, (TOKENS, D), jnp.float32), -5.0, 5.0)
    row_scale = 1.0 + 2.0 * row_frac
    return (values * row_scale).astype(jnp.bfloat16)


def packed_layout(key):
    sequences = TOKENS // SEQ_LEN
    doc_slots = SEQ_LEN // DOC_MIN + 1
    doc_lengths = jax.random.randint(jax.random.fold_in(key, 1), (sequences, doc_slots), DOC_MIN, DOC_MAX + 1)
    chosen = jax.random.randint(jax.random.fold_in(key, 2), (), 0, sequences)
    offset = jax.random.randint(jax.random.fold_in(key, 3), (), 0, max(sequences - 1, 1))
    short_seq = (chosen + 1 + offset) % sequences
    seq_index = jnp.arange(sequences)[:, None]
    slot_order = jnp.arange(doc_slots)[None, :]
    doc_lengths = jnp.where(seq_index == short_seq, DOC_MIN, doc_lengths)
    doc_lengths = jnp.where((seq_index == chosen) & (slot_order == 0), DOC_MAX, doc_lengths).astype(jnp.int32)
    doc_ends = jnp.cumsum(doc_lengths, axis=1)
    doc_starts = doc_ends - doc_lengths
    fit_count = jnp.sum((doc_ends <= SEQ_LEN).astype(jnp.int32), axis=1)
    slot_index = jnp.arange(SEQ_LEN, dtype=jnp.int32)
    doc_index = jnp.sum((doc_ends[:, None, :] <= slot_index[None, :, None]).astype(jnp.int32), axis=2)
    onehot = doc_index[:, :, None] == jnp.arange(doc_slots)[None, None, :]
    start_token = jnp.sum(jnp.where(onehot, doc_starts[:, None, :], 0), axis=2)
    segment_ids = jnp.where(doc_index < fit_count[:, None], doc_index, -1)
    position_ids = jnp.where(segment_ids >= 0, slot_index[None, :] - start_token, 0)
    return (segment_ids.reshape(-1).astype(jnp.int32), position_ids.reshape(-1).astype(jnp.int32))


def draw_segments(key, part):
    return packed_layout(jax.random.fold_in(key, 7))[0]


def draw_positions(key, part):
    return packed_layout(jax.random.fold_in(key, 7))[1]


def strengthened(values, rng, source, target, blocks, factor):
    def block_of(dim):
        return (jnp.arange(values.shape[dim]) // (values.shape[dim] // blocks)).reshape((-1,) + (1,) * (values.ndim - 1 - dim))

    near = jax.random.permutation(rng, blocks)[block_of(target)]
    second = (block_of(target) + blocks // 2) % blocks
    return jnp.where((block_of(source) == near) | (block_of(source) == second), factor * values, values)


def block_scale(key, extent, split, low, top_value):
    def one(dim, shards_of):
        draws = jax.random.uniform(jax.random.fold_in(jax.random.fold_in(key, 6), dim), (shards_of,), jnp.float32, low / len(split), top_value / len(split))
        return jnp.repeat(jnp.exp(draws), extent[dim] // shards_of).reshape((-1,) + (1,) * (len(extent) - dim - 1))

    loudness = one(*split[0])
    for cut in split[1:]:
        loudness = loudness * one(*cut)
    return loudness


def normal_values(own_key, shape, width, limit, split=(), kind=jnp.bfloat16):
    gain = block_scale(own_key, shape, split, -0.22, 0.18) if split else 1.0
    drawn = jax.random.normal(own_key, shape, jnp.float32) * width * gain
    return jnp.minimum(jnp.maximum(drawn, -limit), limit).astype(kind)


def heavy_noise(rng, extent, width, most, cuts, heavy, kind=jnp.bfloat16):
    values = width * jax.random.normal(rng, extent, jnp.float32)
    if cuts:
        values = values * block_scale(rng, extent, cuts, -0.22, 0.18)
    return jnp.clip(strengthened(values, jax.random.fold_in(rng, 3), *heavy), -most, most).astype(kind)


def setup_inputs(seed: int = 0) -> dict:
    keys = jax.random.split(jax.random.key(seed), 13)
    residual_in = draw_residual_in(jax.random.fold_in(keys[12], 71), 0)
    segments = draw_segments(jax.random.fold_in(keys[12], 71), 0)
    positions = draw_positions(jax.random.fold_in(keys[12], 71), 0)
    query_weight = normal_values(keys[3], (D, D), D ** -0.5, 0.1875, ((0, 8), (1, 4)))
    key_weight = normal_values(keys[4], (D, D), D ** -0.5, 0.1875, ((0, 8), (1, 4)))
    value_weight = normal_values(keys[5], (D, D), D ** -0.5, 0.1875, ((0, 8), (1, 4)))
    out_weight = normal_values(keys[6], (D, D), (D // 16) ** -0.5, 0.75, ((0, 8), (1, 4)))
    up_weight = normal_values(keys[7], (D, FF), D ** -0.5, 0.1875, ((0, 8), (1, 4)))
    down_weight = normal_values(keys[8], (D, FF), FF ** -0.5, 0.09375, ((0, 8), (1, 4)))
    norm_gains = jnp.clip(1.0 + 0.15 * jax.random.normal(keys[9], (4, D), jnp.float32), 0.25, 1.75)
    norm_biases = normal_values(keys[10], (4, D), 0.2, 1.0, ((1, 32),), jnp.float32)
    cotangent = heavy_noise(keys[11], (TOKENS, D), 1.0, 6.0, ((0, 32),), (0, 1, 32, 2.75))
    return {"residual_in": residual_in, "segments": segments, "positions": positions, "query_weight": query_weight, "key_weight": key_weight, "value_weight": value_weight, "out_weight": out_weight, "up_weight": up_weight, "down_weight": down_weight, "norm_gains": norm_gains, "norm_biases": norm_biases, "cotangent": cotangent}


EPSILON = 1e-05
MASKED = -1e+30
ROPE_BASE = 10000.0
HIGHEST = lax.Precision.HIGHEST

@jax.custom_vjp
def low(v):
    return lax.optimization_barrier(v.astype(jnp.bfloat16)).astype(jnp.float32)

@jax.custom_vjp
def low_back(v):
    return v

def low_keep(v):
    return (low(v), None)

def low_pass(kept, grad):
    return (grad,)

def back_keep(v):
    return (v, None)

def back_low(kept, grad):
    return (low(grad),)
low.defvjp(low_keep, low_pass)
low_back.defvjp(back_keep, back_low)

def matmul(left, right):
    return jnp.dot(left, right, precision=HIGHEST, preferred_element_type=jnp.float32)

def layer_norm(values, gain_row, bias_row):
    row_mean = lax.optimization_barrier(jnp.mean(values, axis=-1, keepdims=True))
    centred = values - row_mean
    variance = lax.optimization_barrier(jnp.mean(centred * centred, axis=-1, keepdims=True))
    return centred * lax.rsqrt(variance + EPSILON) * gain_row + bias_row

def rotary_tables(position_rows):
    half_size = HEAD_DIM // 2
    inv_freqs = jnp.exp(jnp.arange(half_size, dtype=jnp.float32) * (-2.0 * math.log(ROPE_BASE) / HEAD_DIM))
    angles = position_rows.astype(jnp.float32)[:, None] * inv_freqs[None, :]
    return (jnp.cos(angles)[:, None, :], jnp.sin(angles)[:, None, :])

def rotate(values, cos_table, sin_table):
    half_size = values.shape[-1] // 2
    front_half = values[..., :half_size]
    back_half = values[..., half_size:]
    return jnp.concatenate([front_half * cos_table - back_half * sin_table, back_half * cos_table + front_half * sin_table], axis=-1)

def key_allowed(segment_row):
    row_order = jnp.arange(segment_row.shape[0])
    return (segment_row[:, None] == segment_row[None, :]) & (row_order[None, :] <= row_order[:, None])

def attend_sequence(block_items):
    queries, keys_in, values_in, segment_row = block_items
    scores = jnp.einsum('qhd,khd->hqk', queries, keys_in, precision=HIGHEST) * (1.0 / math.sqrt(HEAD_DIM))
    scores = low_back(scores)
    scores = jnp.where(key_allowed(segment_row)[None], scores, MASKED)
    attn_probs = low(jax.nn.softmax(scores, axis=-1))
    return jnp.einsum('hqk,khd->qhd', attn_probs, values_in, precision=HIGHEST)

def block_forward(params, inputs, segment_rows, position_rows):
    query_weight, key_weight, value_weight, out_weight, up_weight, down_weight, gains, biases = params
    rows_here = inputs.shape[0]
    heads_all = D // HEAD_DIM
    valid_rows = (segment_rows >= 0).astype(jnp.float32)[:, None]
    attn_in = low(layer_norm(inputs, gains[0], biases[0]))
    cos_table, sin_table = rotary_tables(position_rows)
    shaped = (rows_here, heads_all, HEAD_DIM)
    queries = low(rotate(low_back(matmul(attn_in, query_weight)).reshape(shaped), cos_table, sin_table))
    keys_rot = low(rotate(low_back(matmul(attn_in, key_weight)).reshape(shaped), cos_table, sin_table))
    values_rows = low(low_back(matmul(attn_in, value_weight))).reshape(shaped)
    seq_shape = (rows_here // SEQ_LEN, SEQ_LEN, heads_all, HEAD_DIM)
    attended = lax.map(jax.checkpoint(attend_sequence), (queries.reshape(seq_shape), keys_rot.reshape(seq_shape), values_rows.reshape(seq_shape), segment_rows.reshape(-1, SEQ_LEN)))
    attended = low(low_back(attended.reshape(rows_here, D)))
    raw_attn = low_back(matmul(attended, out_weight.T))
    hidden_res = inputs + layer_norm(raw_attn, gains[1], biases[1])
    mlp_in = low(layer_norm(hidden_res, gains[2], biases[2]))
    up_values = low_back(matmul(mlp_in, up_weight))
    activated = low(jax.nn.gelu(up_values, approximate=True))
    raw_mlp = low_back(matmul(activated, down_weight.T))
    block_out = hidden_res + layer_norm(raw_mlp, gains[3], biases[3])
    squares = jnp.stack([jnp.sum(inputs * inputs * valid_rows), jnp.sum(raw_attn * raw_attn * valid_rows), jnp.sum(raw_mlp * raw_mlp * valid_rows), jnp.sum(valid_rows)])
    return (block_out, squares)

def reference(residual_in, segments, positions, query_weight, key_weight, value_weight, out_weight, up_weight, down_weight, norm_gains, norm_biases, cotangent):
    blocks = N_DP
    block_rows = TOKENS // blocks
    params = (query_weight.astype(jnp.float32), key_weight.astype(jnp.float32), value_weight.astype(jnp.float32), out_weight.astype(jnp.float32), up_weight.astype(jnp.float32), down_weight.astype(jnp.float32), norm_gains, norm_biases)
    inputs = residual_in.astype(jnp.float32).reshape(blocks, block_rows, D)
    segment_blocks = segments.reshape(blocks, block_rows)
    position_blocks = positions.reshape(blocks, block_rows)

    def forward_all(params_in, inputs_in):

        def scan_step(running, block_items):
            block_in, segment_rows, position_rows = block_items
            block_out, squares = jax.checkpoint(block_forward)(params_in, block_in, segment_rows, position_rows)
            return (running + squares, block_out)
        totals, outputs = lax.scan(scan_step, jnp.zeros((4,), jnp.float32), (inputs_in, segment_blocks, position_blocks))
        return (outputs, totals)
    outputs, pullback, totals = jax.vjp(forward_all, params, inputs, has_aux=True)
    valid_rows = (segment_blocks >= 0).astype(jnp.float32)[..., None]
    upstream = cotangent.astype(jnp.float32).reshape(blocks, block_rows, D) * valid_rows
    param_grads, input_grads = pullback(upstream)
    grad_scale = 1.0 / math.sqrt(TOKENS)
    rms_values = jnp.sqrt(totals[:3] / (totals[3] * D))
    return (outputs.reshape(TOKENS, D).astype(jnp.bfloat16), input_grads.reshape(TOKENS, D).astype(jnp.bfloat16), param_grads[0] * grad_scale, param_grads[1] * grad_scale, param_grads[2] * grad_scale, param_grads[3] * grad_scale, param_grads[4] * grad_scale, param_grads[5] * grad_scale, param_grads[6] * grad_scale, param_grads[7] * grad_scale, rms_values)
```

```python
import math

import jax
import jax.numpy as jnp
from jax import lax
from jax.sharding import PartitionSpec as P

D = 1024
HEAD_DIM = 64
SEQ_LEN = 1024

EPSILON = 1e-05
MASKED = -1e30
ROPE_BASE = 10000.0


AXES = ("dp", "tensor")
Z_LO, Z_HI, CORE = 1, 2, 4
OUTER_BIT = 3
PIECES = (0, 2, 1, 3)


def device_count():
    return lax.axis_size("dp") * lax.axis_size("tensor")


def exchange(values, mask):
    pairs = [(i, i ^ mask) for i in range(device_count())]
    return lax.ppermute(values, AXES, pairs)


def move_tokens(values):
    def target(i):
        core, z_hi = (i >> 2) & 1, (i >> 1) & 1
        return i if core == z_hi else i ^ (Z_HI | CORE)

    return lax.ppermute(values, AXES, [(i, target(i)) for i in range(device_count())])


def sum_everywhere(values):
    for bit in range(device_count().bit_length() - 1):
        values = values + exchange(values, 1 << bit)
    return values


def gather_rows(own):
    across = exchange(own, Z_LO)
    beside = exchange(own, CORE)
    return jnp.concatenate([own, beside, across, exchange(across, CORE)], axis=0)


def sum_rows(partial_sums):
    own, beside, across, both = jnp.split(partial_sums, 4, axis=0)
    far = across + exchange(both.astype(jnp.bfloat16), CORE).astype(jnp.float32)
    far = exchange(far.astype(jnp.bfloat16), Z_LO).astype(jnp.float32)
    near = own + exchange(beside.astype(jnp.bfloat16), CORE).astype(jnp.float32)
    return near + far


class Place:
    def __init__(self):
        self.dp = lax.axis_index("dp")
        self.tensor = lax.axis_index("tensor")
        self.core = self.dp % 2
        self.outer = self.dp // 2
        self.z_lo = self.tensor % 2
        self.z_hi = self.tensor // 2
        self.chunk = 2 * self.core + self.z_lo
        self.at_home = self.core == self.z_hi
        self.outer_bits = (lax.axis_size("dp") // 2).bit_length() - 1


def pick(values, axis, index):
    return lax.dynamic_index_in_dim(values, index, axis, keepdims=False)


def gather_weight(block, place, bits):
    rows, columns = block.shape
    other = exchange(block, Z_HI)
    keep = jnp.where(place.at_home, block, other)
    got = exchange(jnp.where(place.at_home, other, block), CORE)
    held = jnp.where(
        place.core == 0, jnp.concatenate([keep, got]), jnp.concatenate([got, keep])
    )[None]
    for bit in bits:
        held = jnp.concatenate([held, exchange(held, 1 << (OUTER_BIT + bit))])
    parts = []
    for k in range(held.shape[0]):
        label = k ^ place.outer
        index = sum(((label >> bit) & 1) << step for step, bit in enumerate(bits))
        parts.append(pick(held, 0, index))
    return jnp.concatenate(parts)


def reduce_weight(left, right, place, bits):
    tokens = left.shape[0]
    count = place.outer_bits
    shaped = left.reshape((tokens,) + (2,) * count + (left.shape[1] >> count,))
    axes = list(range(count - 1, -1, -1))
    first = 1 + axes.index(bits[0])
    mine = (place.outer >> bits[0]) & 1

    def product(half):
        return outer_sum(pick(shaped, first, half).reshape(tokens, -1), right)

    sent = exchange(product(1 - mine).astype(jnp.bfloat16), 1 << (OUTER_BIT + bits[0]))
    total = product(mine) + sent.astype(jnp.float32)
    axes.remove(bits[0])
    total = total.reshape((2,) * (count - 1) + (-1, total.shape[-1]))
    for bit in bits[1:]:
        mine = (place.outer >> bit) & 1
        axis = axes.index(bit)
        sent = pick(total, axis, 1 - mine).astype(jnp.bfloat16)
        sent = exchange(sent, 1 << (OUTER_BIT + bit)).astype(jnp.float32)
        total = pick(total, axis, mine) + sent
        axes.remove(bit)
    total = total.reshape(2, -1, total.shape[-1])
    keep = pick(total, 0, place.core)
    got = exchange(pick(total, 0, 1 - place.core).astype(jnp.bfloat16), CORE)
    got = got.astype(jnp.float32)
    sent = jnp.where(place.at_home, got, keep).astype(jnp.bfloat16)
    return jnp.where(place.at_home, keep, got) + exchange(sent, Z_HI).astype(jnp.float32)


def layer_norm(values, gain_row, bias_row):
    row_mean = jnp.mean(values, axis=-1, keepdims=True)
    centred = values - row_mean
    variance = jnp.mean(centred * centred, axis=-1, keepdims=True)
    inv_std = lax.rsqrt(variance + EPSILON)
    normed = centred * inv_std
    return (normed * gain_row + bias_row, (normed, inv_std))


def norm_backward(upstream, saved_stats, gain_row):
    normed, inv_std = saved_stats
    scaled = upstream * gain_row
    first_mean = jnp.mean(scaled, axis=-1, keepdims=True)
    cross_mean = jnp.mean(scaled * normed, axis=-1, keepdims=True)
    inputs_grad = inv_std * (scaled - first_mean - normed * cross_mean)
    return (inputs_grad, jnp.sum(upstream * normed, axis=0), jnp.sum(upstream, axis=0))


def gelu_tanh(values):
    return jax.nn.gelu(values, approximate=True)


def rotary_tables(position_rows, head_size):
    half_size = head_size // 2
    inv_freqs = jnp.exp(
        jnp.arange(half_size, dtype=jnp.float32) * (-2.0 * math.log(ROPE_BASE) / head_size)
    )
    angles = position_rows.astype(jnp.float32)[:, None] * inv_freqs[None, :]
    return (jnp.cos(angles)[:, None, :], jnp.sin(angles)[:, None, :])


def rotate(values, cos_table, sin_table):
    half_size = values.shape[-1] // 2
    front_half = values[..., :half_size]
    back_half = values[..., half_size:]
    return jnp.concatenate(
        [
            front_half * cos_table - back_half * sin_table,
            back_half * cos_table + front_half * sin_table,
        ],
        axis=-1,
    )


def masked_scores(queries, keys_in, allowed):
    scores = jnp.einsum("qhd,khd->hqk", queries, keys_in, preferred_element_type=jnp.float32) * (
        1.0 / math.sqrt(queries.shape[-1])
    )
    return jnp.where(allowed[None], scores, MASKED)


def attend_forward(queries, keys_in, values_in, allowed):
    scores = masked_scores(queries, keys_in, allowed)
    row_top = jnp.max(scores, axis=-1, keepdims=True)
    expo = jnp.exp(scores - row_top)
    row_total = jnp.sum(expo, axis=-1, keepdims=True)
    attn_probs = (expo / row_total).astype(jnp.bfloat16)
    attended = jnp.einsum("hqk,khd->qhd", attn_probs, values_in, preferred_element_type=jnp.float32)
    return (attended.astype(jnp.bfloat16), (row_top + jnp.log(row_total))[..., 0])


def attend_backward(queries, keys_in, values_in, allowed, log_total, grad_attended):
    scale_factor = 1.0 / math.sqrt(queries.shape[-1])
    scores = masked_scores(queries, keys_in, allowed)
    attn_probs = jnp.exp(scores - log_total[..., None])
    grad_values = jnp.einsum(
        "hqk,qhd->khd",
        attn_probs.astype(jnp.bfloat16),
        grad_attended,
        preferred_element_type=jnp.float32,
    )
    grad_probs = jnp.einsum(
        "qhd,khd->hqk", grad_attended, values_in, preferred_element_type=jnp.float32
    )
    row_delta = jnp.sum(attn_probs * grad_probs, axis=-1, keepdims=True)
    grad_scores = (attn_probs * (grad_probs - row_delta)).astype(jnp.bfloat16)
    grad_queries = (
        jnp.einsum("hqk,khd->qhd", grad_scores, keys_in, preferred_element_type=jnp.float32)
        * scale_factor
    )
    grad_keys = (
        jnp.einsum("hqk,qhd->khd", grad_scores, queries, preferred_element_type=jnp.float32)
        * scale_factor
    )
    return (grad_queries, grad_keys, grad_values.astype(jnp.bfloat16))


def project(left, right):
    return jnp.dot(left, right, preferred_element_type=jnp.float32)


def project_back(left, right):
    return lax.dot_general(
        left, right, (((1,), (1,)), ((), ())), preferred_element_type=jnp.float32
    )


def outer_sum(left, right):
    return lax.dot_general(
        left, right, (((0,), (0,)), ((), ())), preferred_element_type=jnp.float32
    )


def per_device(
    residual_in,
    segments,
    positions,
    query_weight,
    key_weight,
    value_weight,
    out_weight,
    up_weight,
    down_weight,
    norm_gains,
    norm_biases,
    cotangent,
):
    place = Place()
    local_rows = residual_in.shape[0]
    group_rows = segments.shape[0]
    head_size = HEAD_DIM
    grad_scale = 1.0 / math.sqrt(group_rows * lax.axis_size("dp"))
    up_bits = tuple(range(place.outer_bits))
    down_bits = up_bits[::-1]

    residual_rows = move_tokens(residual_in)
    numbers = jnp.stack([segments, positions])
    numbers = jnp.where(place.at_home, numbers, exchange(numbers, CORE))
    numbers = numbers.reshape(2, 4, local_rows)
    numbers = jnp.stack([pick(numbers, 1, place.chunk ^ p) for p in PIECES], axis=1)
    segment_row, position_row = numbers.reshape(2, group_rows)
    order = jnp.concatenate(
        [(place.chunk ^ p) * local_rows + jnp.arange(local_rows) for p in PIECES]
    )
    allowed = (segment_row[:, None] == segment_row[None, :]) & (order[None, :] <= order[:, None])
    local_valid = (segment_row[:local_rows] >= 0).astype(jnp.float32)[:, None]
    valid_count = jnp.sum(local_valid)

    params = jnp.concatenate([norm_gains, norm_biases])
    width = params.shape[1]
    params = lax.dynamic_update_slice(
        jnp.zeros((params.shape[0], D), jnp.float32),
        params,
        (0, (place.dp * lax.axis_size("tensor") + place.tensor) * width),
    )
    params = sum_everywhere(params)
    gains, biases = params[:4], params[4:]

    qkv_full = gather_weight(
        jnp.concatenate([query_weight, key_weight, value_weight], axis=1), place, up_bits
    )
    out_full = gather_weight(out_weight, place, up_bits)
    up_full = gather_weight(up_weight, place, down_bits)
    down_full = gather_weight(down_weight, place, up_bits)
    head_width = query_weight.shape[1]
    query_full, key_full, value_full = jnp.split(qkv_full, 3, axis=1)

    inputs = residual_rows.astype(jnp.float32)
    input_squares = jnp.sum(inputs * inputs * local_valid)
    attn_in, attn_norm = layer_norm(inputs, gains[0], biases[0])
    attn_rows = gather_rows(attn_in.astype(jnp.bfloat16))
    heads_local = head_width // head_size
    cos_table, sin_table = rotary_tables(position_row, head_size)
    shaped = (group_rows, heads_local, head_size)
    query_rot = rotate(
        project(attn_rows, query_full).reshape(shaped), cos_table, sin_table
    ).astype(jnp.bfloat16)
    key_rot = rotate(project(attn_rows, key_full).reshape(shaped), cos_table, sin_table).astype(
        jnp.bfloat16
    )
    value_rows = project(attn_rows, value_full).astype(jnp.bfloat16).reshape(shaped)
    attended, log_totals = attend_forward(query_rot, key_rot, value_rows, allowed)
    attended = attended.reshape(group_rows, head_width)
    raw_attn = sum_rows(project_back(attended, out_full))
    attn_norm_out, attn_post = layer_norm(raw_attn, gains[1], biases[1])
    hidden_res = inputs + attn_norm_out
    attn_squares = jnp.sum(raw_attn * raw_attn * local_valid)
    mlp_in, mlp_norm = layer_norm(hidden_res, gains[2], biases[2])
    mlp_rows = gather_rows(mlp_in.astype(jnp.bfloat16))
    up_values = project(mlp_rows, up_full)
    activated = gelu_tanh(up_values).astype(jnp.bfloat16)
    raw_mlp = sum_rows(project_back(activated, down_full))
    mlp_norm_out, mlp_post = layer_norm(raw_mlp, gains[3], biases[3])
    layer_out = move_tokens((hidden_res + mlp_norm_out).astype(jnp.bfloat16))
    mlp_squares = jnp.sum(raw_mlp * raw_mlp * local_valid)

    upstream = move_tokens(cotangent).astype(jnp.float32) * local_valid
    grad_raw_mlp, gain_three, bias_three = norm_backward(upstream, mlp_post, gains[3])
    grad_mlp_rows = gather_rows(grad_raw_mlp.astype(jnp.bfloat16))
    grad_act = project(grad_mlp_rows, down_full)
    grad_up = jax.vjp(gelu_tanh, up_values)[1](grad_act)[0].astype(jnp.bfloat16)
    grad_mlp_in = sum_rows(project_back(grad_up, up_full))
    grad_up_weight = reduce_weight(mlp_rows, grad_up, place, up_bits)
    grad_down_weight = reduce_weight(grad_mlp_rows, activated, place, down_bits)
    grad_hidden_part, gain_two, bias_two = norm_backward(grad_mlp_in, mlp_norm, gains[2])
    grad_hidden = upstream + grad_hidden_part
    grad_raw_attn, gain_one, bias_one = norm_backward(grad_hidden, attn_post, gains[1])
    grad_attn_rows = gather_rows(grad_raw_attn.astype(jnp.bfloat16))
    grad_attended = project(grad_attn_rows, out_full).astype(jnp.bfloat16)
    grad_out_weight = reduce_weight(grad_attn_rows, attended, place, down_bits)
    grad_queries, grad_keys, grad_values = attend_backward(
        query_rot, key_rot, value_rows, allowed, log_totals, grad_attended.reshape(shaped)
    )
    grad_queries = (
        rotate(grad_queries, cos_table, -sin_table).reshape(group_rows, -1).astype(jnp.bfloat16)
    )
    grad_keys = (
        rotate(grad_keys, cos_table, -sin_table).reshape(group_rows, -1).astype(jnp.bfloat16)
    )
    grad_qkv = jnp.concatenate(
        [grad_queries, grad_keys, grad_values.reshape(group_rows, -1)], axis=1
    )
    grad_qkv_weight = reduce_weight(attn_rows, grad_qkv, place, up_bits)
    grad_attn_in = sum_rows(project_back(grad_qkv, qkv_full))
    grad_input_part, gain_zero, bias_zero = norm_backward(grad_attn_in, attn_norm, gains[0])
    grad_input = move_tokens((grad_hidden + grad_input_part).astype(jnp.bfloat16))
    stats = jnp.stack([input_squares, attn_squares, mlp_squares, valid_count])
    totals = jnp.stack(
        [
            gain_zero,
            gain_one,
            gain_two,
            gain_three,
            bias_zero,
            bias_one,
            bias_two,
            bias_three,
            jnp.pad(stats, (0, D - 4)),
        ]
    )
    totals = sum_everywhere(totals)
    norm_grads = (
        lax.dynamic_slice(
            totals, (0, (place.dp * lax.axis_size("tensor") + place.tensor) * width), (8, width)
        )
        * grad_scale
    )
    rms_values = jnp.sqrt(totals[8, :3] / (totals[8, 3] * D))
    attn_grads = jnp.split(grad_qkv_weight * grad_scale, 3, axis=1)
    return (
        layer_out,
        grad_input,
        *attn_grads,
        grad_out_weight * grad_scale,
        grad_up_weight * grad_scale,
        grad_down_weight * grad_scale,
        norm_grads[:4],
        norm_grads[4:],
        rms_values,
    )


def solution(mesh):
    in_specs = (
        P(("dp", "tensor"), None),
        P("dp"),
        P("dp"),
        P("dp", "tensor"),
        P("dp", "tensor"),
        P("dp", "tensor"),
        P("dp", "tensor"),
        P("dp", "tensor"),
        P("dp", "tensor"),
        P(None, ("dp", "tensor")),
        P(None, ("dp", "tensor")),
        P(("dp", "tensor"), None),
    )
    out_specs = (
        P(("dp", "tensor"), None),
        P(("dp", "tensor"), None),
        P("dp", "tensor"),
        P("dp", "tensor"),
        P("dp", "tensor"),
        P("dp", "tensor"),
        P("dp", "tensor"),
        P("dp", "tensor"),
        P(None, ("dp", "tensor")),
        P(None, ("dp", "tensor")),
        P(),
    )
    return jax.shard_map(
        per_device, mesh=mesh, in_specs=in_specs, out_specs=out_specs, check_vma=False
    )
```

```python
import functools
import math

import jax
import jax.numpy as jnp
from jax import lax
from jax.experimental import pallas as pl
from jax.experimental.pallas import tpu as pltpu
from jax.sharding import PartitionSpec as P

D = 1024
HEAD_DIM = 64
SEQ_LEN = 1024

EPSILON = 1e-05
MASKED = -1e30
ROPE_BASE = 10000.0

CHUNKS = 4

AXES = ("dp", "tensor")
Z_LO, Z_HI, CORE = 1, 2, 4
OUTER_BIT = 3
PIECES = (0, 2, 1, 3)


def device_count():
    return lax.axis_size("dp") * lax.axis_size("tensor")


def exchange(values, mask):
    pairs = [(i, i ^ mask) for i in range(device_count())]
    return lax.ppermute(values, AXES, pairs)


def move_tokens(values):
    def target(i):
        core, z_hi = (i >> 2) & 1, (i >> 1) & 1
        return i if core == z_hi else i ^ (Z_HI | CORE)

    return lax.ppermute(values, AXES, [(i, target(i)) for i in range(device_count())])


def sum_everywhere(values):
    bits = device_count().bit_length() - 1
    values = values + exchange(values, CORE)
    masks = [1 << bit for bit in range(bits) if 1 << bit != CORE]
    for first, second in zip(masks[::2], masks[1::2]):
        values = (values + exchange(values, first)) + (
            exchange(values, second) + exchange(values, first | second)
        )
    if len(masks) % 2:
        values = values + exchange(values, masks[-1])
    return values


def after(values, earlier):
    return lax.optimization_barrier((values, earlier))[0]


def gather_rows(own):
    across = exchange(own, Z_LO)
    beside = exchange(own, CORE)
    near = jnp.concatenate([own, beside])
    return (near, jnp.concatenate([across, exchange(across, CORE)]))


def sum_rows(near_rows, far_rows):
    own, beside = jnp.split(near_rows, 2)
    across, both = jnp.split(far_rows, 2)
    far = across + exchange(both.astype(jnp.bfloat16), CORE).astype(jnp.float32)
    far = exchange(far.astype(jnp.bfloat16), Z_LO).astype(jnp.float32)
    near = own + exchange(beside.astype(jnp.bfloat16), CORE).astype(jnp.float32)
    return near + far


class Place:
    def __init__(self):
        self.dp = lax.axis_index("dp")
        self.tensor = lax.axis_index("tensor")
        self.core = self.dp % 2
        self.outer = self.dp // 2
        self.z_lo = self.tensor % 2
        self.z_hi = self.tensor // 2
        self.chunk = 2 * self.core + self.z_lo
        self.at_home = self.core == self.z_hi
        self.outer_bits = (lax.axis_size("dp") // 2).bit_length() - 1


def pick(values, axis, index):
    return lax.dynamic_index_in_dim(values, index, axis, keepdims=False)


def gather_weight(block, other, place, bits):
    keep = jnp.where(place.at_home, block, other)
    got = exchange(jnp.where(place.at_home, other, block), CORE)
    held = jnp.where(
        place.core == 0, jnp.concatenate([keep, got]), jnp.concatenate([got, keep])
    )[None]
    for bit in bits:
        held = jnp.concatenate([held, exchange(held, 1 << (OUTER_BIT + bit))])
    parts = []
    for k in range(held.shape[0]):
        label = k ^ place.outer
        index = sum(((label >> bit) & 1) << step for step, bit in enumerate(bits))
        parts.append(pick(held, 0, index))
    return jnp.concatenate(parts)


def reduce_weight(lefts, rights, place, bits):
    tokens = lefts[0].shape[0]
    count = place.outer_bits
    axes = list(range(count - 1, -1, -1))
    first = 1 + axes.index(bits[0])
    mine = (place.outer >> bits[0]) & 1

    def product(half):
        total = 0.0
        for left, right in zip(lefts, rights):
            left = left.reshape((tokens,) + (2,) * count + (left.shape[1] >> count,))
            total = total + outer_sum(pick(left, first, half).reshape(tokens, -1), right)
        return total

    sent = exchange(product(1 - mine).astype(jnp.bfloat16), 1 << (OUTER_BIT + bits[0]))
    total = product(mine) + sent.astype(jnp.float32)
    axes.remove(bits[0])
    total = total.reshape((2,) * (count - 1) + (-1, total.shape[-1]))
    for bit in bits[1:]:
        mine = (place.outer >> bit) & 1
        axis = axes.index(bit)
        sent = pick(total, axis, 1 - mine).astype(jnp.bfloat16)
        sent = exchange(sent, 1 << (OUTER_BIT + bit)).astype(jnp.float32)
        total = pick(total, axis, mine) + sent
        axes.remove(bit)
    total = total.reshape(2, -1, total.shape[-1])
    keep = pick(total, 0, place.core)
    got = exchange(pick(total, 0, 1 - place.core).astype(jnp.bfloat16), CORE)
    got = got.astype(jnp.float32)
    sent = jnp.where(place.at_home, got, keep).astype(jnp.bfloat16)
    return jnp.where(place.at_home, keep, got) + exchange(sent, Z_HI).astype(jnp.float32)


def layer_norm(values, gain_row, bias_row):
    row_mean = jnp.mean(values, axis=-1, keepdims=True)
    centred = values - row_mean
    variance = jnp.mean(centred * centred, axis=-1, keepdims=True)
    inv_std = lax.rsqrt(variance + EPSILON)
    normed = centred * inv_std
    return (normed * gain_row + bias_row, (normed, inv_std))


def norm_backward(upstream, saved_stats, gain_row):
    normed, inv_std = saved_stats
    scaled = upstream * gain_row
    first_mean = jnp.mean(scaled, axis=-1, keepdims=True)
    cross_mean = jnp.mean(scaled * normed, axis=-1, keepdims=True)
    inputs_grad = inv_std * (scaled - first_mean - normed * cross_mean)
    return (inputs_grad, jnp.sum(upstream * normed, axis=0), jnp.sum(upstream, axis=0))


def gelu_tanh(values):
    return jax.nn.gelu(values, approximate=True)


def rotary_tables(position_rows, head_size):
    half_size = head_size // 2
    inv_freqs = jnp.exp(
        jnp.arange(half_size, dtype=jnp.float32) * (-2.0 * math.log(ROPE_BASE) / head_size)
    )
    angles = position_rows.astype(jnp.float32)[:, None] * inv_freqs[None, :]
    return (jnp.cos(angles)[:, None, :], jnp.sin(angles)[:, None, :])


def rotate(values, cos_table, sin_table):
    half_size = values.shape[-1] // 2
    front_half = values[..., :half_size]
    back_half = values[..., half_size:]
    return jnp.concatenate(
        [
            front_half * cos_table - back_half * sin_table,
            back_half * cos_table + front_half * sin_table,
        ],
        axis=-1,
    )


def dot_nt(left, right):
    return lax.dot_general(
        left, right, (((1,), (1,)), ((), ())), preferred_element_type=jnp.float32
    )


def dot_nn(left, right):
    return jnp.dot(left, right, preferred_element_type=jnp.float32)


def head_lanes(values, head):
    lanes = lax.broadcasted_iota(jnp.int32, values.shape, 1) // HEAD_DIM
    return jnp.where(lanes == head, values, jnp.zeros_like(values))


def fill_bias(bias_ref, key_segments, query_segments, j, size):
    query_row = query_segments[:, j * size : (j + 1) * size]
    for i in range(j + 1):
        same = key_segments[i * size : (i + 1) * size, :1] == query_row
        if i == j:
            key_at = lax.broadcasted_iota(jnp.int32, (size, size), 0)
            query_at = lax.broadcasted_iota(jnp.int32, (size, size), 1)
            same = same & (key_at <= query_at)
        bias_ref[i] = jnp.where(same, 0.0, MASKED)


def in_order(chunks, near_ref, far_ref, held_ref):
    size = near_ref.shape[0] // 2
    for s in range(CHUNKS):
        source = near_ref if s < 2 else far_ref
        held_ref[pl.ds(pl.multiple_of(chunks[s] * size, size), size), :] = source[
            (s % 2) * size : (s % 2 + 1) * size, :
        ]


def in_pieces(chunks, held_ref, near_ref, far_ref):
    size = near_ref.shape[0] // 2
    for s in range(CHUNKS):
        target = near_ref if s < 2 else far_ref
        target[(s % 2) * size : (s % 2 + 1) * size, :] = held_ref[
            pl.ds(pl.multiple_of(chunks[s] * size, size), size), :
        ].astype(target.dtype)


def attend_kernel(
    chunks, qn, qf, kn, kf, vn, vf, key_segments, query_segments,
    out_near, out_far, lse_ref, q_all, k_all, v_all, vt_ref, ot_ref, out_all, bias_ref,
):
    in_order(chunks, qn, qf, q_all)
    in_order(chunks, kn, kf, k_all)
    in_order(chunks, vn, vf, v_all)
    size = q_all.shape[0] // CHUNKS
    heads = q_all.shape[1] // HEAD_DIM
    lse_ref[...] = jnp.zeros_like(lse_ref)
    for i in range(CHUNKS):
        here = slice(i * size, (i + 1) * size)
        vt_ref[:, here] = v_all[here, :].T
    for j in range(CHUNKS):
        fill_bias(bias_ref, key_segments, query_segments, j, size)
        mine = slice(j * size, (j + 1) * size)

        def one_head(head):
            query = head_lanes(q_all[mine, :], head) * jnp.bfloat16(HEAD_DIM**-0.5)
            features = slice(head * HEAD_DIM, (head + 1) * HEAD_DIM)
            row = slice(head, head + 1)
            scores = [
                dot_nt(k_all[i * size : (i + 1) * size, :], query) + bias_ref[i]
                for i in range(j + 1)
            ]
            top = functools.reduce(
                jnp.maximum, [jnp.max(s, axis=0, keepdims=True) for s in scores]
            )
            expo = [jnp.exp(s - top) for s in scores]
            total = sum(jnp.sum(e, axis=0, keepdims=True) for e in expo)
            mixed = sum(
                dot_nn(vt_ref[features, i * size : (i + 1) * size], expo[i].astype(jnp.bfloat16))
                for i in range(j + 1)
            )
            ot_ref[features, :] = mixed * (1.0 / total)
            lse_ref[row, mine] = top + jnp.log(total)

        for head in range(heads):
            one_head(head)
        out_all[mine, :] = ot_ref[...].T.astype(out_all.dtype)
    in_pieces(chunks, out_all, out_near, out_far)


def attend_back_kernel(
    chunks, qn, qf, kn, kf, vn, vf, don, dof, on, of, lse_ref, key_segments, query_segments,
    dqn, dqf, dkn, dkf, dvn, dvf,
    q_all, k_all, v_all, do_all, o_all, kt_ref, dqt_ref, delta_ref, bias_ref, dq_sum, dk_sum, dv_sum,
):
    for near, far, held in ((qn, qf, q_all), (kn, kf, k_all), (vn, vf, v_all), (don, dof, do_all), (on, of, o_all)):
        in_order(chunks, near, far, held)
    size = q_all.shape[0] // CHUNKS
    heads = q_all.shape[1] // HEAD_DIM
    for i in range(CHUNKS):
        here = slice(i * size, (i + 1) * size)
        kt_ref[:, here] = k_all[here, :].T
    dk_sum[...] = jnp.zeros_like(dk_sum)
    dv_sum[...] = jnp.zeros_like(dv_sum)
    for j in range(CHUNKS):
        fill_bias(bias_ref, key_segments, query_segments, j, size)
        mine = slice(j * size, (j + 1) * size)
        delta_ref[...] = (
            do_all[mine, :].astype(jnp.float32) * o_all[mine, :].astype(jnp.float32)
        ).T

        def one_head(head):
            query = head_lanes(q_all[mine, :], head) * jnp.bfloat16(HEAD_DIM**-0.5)
            upstream = head_lanes(do_all[mine, :], head)
            features = slice(head * HEAD_DIM, (head + 1) * HEAD_DIM)
            row = slice(head, head + 1)
            delta = jnp.sum(delta_ref[features, :], axis=0, keepdims=True)
            lse = lse_ref[row, mine]
            dqt = jnp.zeros((HEAD_DIM, size), jnp.float32)
            for i in range(j + 1):
                here = slice(i * size, (i + 1) * size)
                probs = jnp.exp(dot_nt(k_all[here, :], query) + bias_ref[i] - lse)
                dprobs = dot_nt(v_all[here, :], upstream)
                dscores = (probs * (dprobs - delta)).astype(jnp.bfloat16)
                dv_sum[here, :] += dot_nn(probs.astype(jnp.bfloat16), upstream)
                dk_sum[here, :] += dot_nn(dscores, query)
                dqt += dot_nn(kt_ref[features, here], dscores)
            dqt_ref[features, :] = dqt

        for head in range(heads):
            one_head(head)
        dq_sum[mine, :] = dqt_ref[...].T * HEAD_DIM**-0.5
    in_pieces(chunks, dq_sum, dqn, dqf)
    in_pieces(chunks, dk_sum, dkn, dkf)
    in_pieces(chunks, dv_sum, dvn, dvf)


VMEM = pl.BlockSpec(memory_space=pltpu.VMEM)
SMEM = pl.BlockSpec(memory_space=pltpu.SMEM)


def halves(tokens, width, kind):
    return [jax.ShapeDtypeStruct((tokens // 2, width), kind)] * 2


def attend_forward(chunks, queries, keys_in, values_in, key_segments, query_segments):
    tokens, width = query_segments.shape[1], queries[0].shape[1]
    size = tokens // CHUNKS
    near, far, lse = pl.pallas_call(
        attend_kernel,
        out_shape=(
            *halves(tokens, width, jnp.bfloat16),
            jax.ShapeDtypeStruct((8, tokens), jnp.float32),
        ),
        in_specs=[SMEM] + [VMEM] * 8,
        out_specs=(VMEM,) * 3,
        scratch_shapes=[pltpu.VMEM((tokens, width), jnp.bfloat16)] * 3
        + [
            pltpu.VMEM((width, tokens), jnp.bfloat16),
            pltpu.VMEM((width, size), jnp.float32),
            pltpu.VMEM((tokens, width), jnp.bfloat16),
            pltpu.VMEM((CHUNKS, size, size), jnp.float32),
        ],
        cost_estimate=pl.CostEstimate(
            flops=4 * tokens * tokens * width,
            bytes_accessed=8 * tokens * width,
            transcendentals=4 * tokens * tokens,
        ),
        name="attend_forward",
    )(chunks, *queries, *keys_in, *values_in, key_segments, query_segments)
    return (near, far), lse


def attend_backward(
    chunks, queries, keys_in, values_in, grad_attended, attended, lse, key_segments, query_segments
):
    tokens, width = query_segments.shape[1], queries[0].shape[1]
    size = tokens // CHUNKS
    grads = pl.pallas_call(
        attend_back_kernel,
        out_shape=(
            *halves(tokens, width, jnp.float32),
            *halves(tokens, width, jnp.float32),
            *halves(tokens, width, jnp.bfloat16),
        ),
        in_specs=[SMEM] + [VMEM] * 13,
        out_specs=(VMEM,) * 6,
        scratch_shapes=[pltpu.VMEM((tokens, width), jnp.bfloat16)] * 5
        + [
            pltpu.VMEM((width, tokens), jnp.bfloat16),
            pltpu.VMEM((width, size), jnp.float32),
            pltpu.VMEM((width, size), jnp.float32),
            pltpu.VMEM((CHUNKS, size, size), jnp.float32),
        ]
        + [pltpu.VMEM((tokens, width), jnp.float32)] * 3,
        cost_estimate=pl.CostEstimate(
            flops=10 * tokens * tokens * width,
            bytes_accessed=16 * tokens * width,
            transcendentals=4 * tokens * tokens,
        ),
        name="attend_backward",
    )(
        chunks, *queries, *keys_in, *values_in, *grad_attended, *attended, lse,
        key_segments, query_segments,
    )
    return grads[:2], grads[2:4], grads[4:]


def project(left, right):
    return jnp.dot(left, right, preferred_element_type=jnp.float32)


def project_back(left, right):
    return lax.dot_general(
        left, right, (((1,), (1,)), ((), ())), preferred_element_type=jnp.float32
    )


def outer_sum(left, right):
    return lax.dot_general(
        left, right, (((0,), (0,)), ((), ())), preferred_element_type=jnp.float32
    )


def per_device(
    residual_in,
    segments,
    positions,
    query_weight,
    key_weight,
    value_weight,
    out_weight,
    up_weight,
    down_weight,
    norm_gains,
    norm_biases,
    cotangent,
):
    place = Place()
    local_rows = residual_in.shape[0]
    group_rows = segments.shape[0]
    head_size = HEAD_DIM
    grad_scale = 1.0 / math.sqrt(group_rows * lax.axis_size("dp"))
    up_bits = tuple(range(place.outer_bits))
    down_bits = up_bits[::-1]

    qkv_block = jnp.concatenate([query_weight, key_weight, value_weight], axis=1)
    residual_rows = move_tokens(residual_in)
    qkv_other = exchange(qkv_block, Z_HI)
    numbers = jnp.stack([segments, positions])
    numbers = jnp.where(place.at_home, numbers, exchange(numbers, CORE))
    query_segments = numbers[:1]
    key_segments = jnp.broadcast_to(numbers[0][:, None], (group_rows, 128))
    numbers = numbers.reshape(2, 4, local_rows)
    numbers = jnp.stack([pick(numbers, 1, place.chunk ^ p) for p in PIECES], axis=1)
    chunks = jnp.stack([place.chunk ^ p for p in PIECES]).astype(jnp.int32)
    local_valid = (numbers[0, 0] >= 0).astype(jnp.float32)[:, None]
    valid_count = jnp.sum(local_valid)
    tables = [
        rotary_tables(half, head_size) for half in numbers[1].reshape(2, 2 * local_rows)
    ]

    params = jnp.concatenate([norm_gains, norm_biases])
    width = params.shape[1]
    params = lax.dynamic_update_slice(
        jnp.zeros((params.shape[0], D), jnp.float32),
        params,
        (0, (place.dp * lax.axis_size("tensor") + place.tensor) * width),
    )
    params = sum_everywhere(params)
    gains, biases = params[:4], params[4:]

    qkv_full = gather_weight(qkv_block, qkv_other, place, up_bits)
    out_block, up_block = after((out_weight, up_weight), (qkv_other, residual_rows))
    out_other, up_other = exchange(out_block, Z_HI), exchange(up_block, Z_HI)
    out_full = gather_weight(out_block, out_other, place, up_bits)
    up_full = gather_weight(up_block, up_other, place, down_bits)
    down_block = after(down_weight, up_other)
    down_other = exchange(down_block, Z_HI)
    down_full = gather_weight(down_block, down_other, place, up_bits)
    cotangent_rows = move_tokens(after(cotangent, down_other))
    head_width = query_weight.shape[1]
    query_full, key_full, value_full = jnp.split(qkv_full, 3, axis=1)

    inputs = residual_rows.astype(jnp.float32)
    input_squares = jnp.sum(inputs * inputs * local_valid)
    attn_in, attn_norm = layer_norm(inputs, gains[0], biases[0])
    attn_rows = gather_rows(attn_in.astype(jnp.bfloat16))
    heads_local = head_width // head_size

    def turned(values, table, sign, kind):
        shaped = values.reshape(values.shape[0], heads_local, head_size)
        return rotate(shaped, table[0], sign * table[1]).reshape(values.shape).astype(kind)

    query_rot = [
        turned(project(rows, query_full), table, 1.0, jnp.bfloat16)
        for rows, table in zip(attn_rows, tables)
    ]
    key_rot = [
        turned(project(rows, key_full), table, 1.0, jnp.bfloat16)
        for rows, table in zip(attn_rows, tables)
    ]
    value_rows = [project(rows, value_full).astype(jnp.bfloat16) for rows in attn_rows]
    attended, log_totals = attend_forward(
        chunks, query_rot, key_rot, value_rows, key_segments, query_segments
    )
    raw_attn = sum_rows(*[project_back(rows, out_full) for rows in attended])
    attn_norm_out, attn_post = layer_norm(raw_attn, gains[1], biases[1])
    hidden_res = inputs + attn_norm_out
    attn_squares = jnp.sum(raw_attn * raw_attn * local_valid)
    mlp_in, mlp_norm = layer_norm(hidden_res, gains[2], biases[2])
    mlp_rows = gather_rows(mlp_in.astype(jnp.bfloat16))
    up_values = [project(rows, up_full) for rows in mlp_rows]
    activated = [gelu_tanh(values).astype(jnp.bfloat16) for values in up_values]
    raw_mlp = sum_rows(*[project_back(rows, down_full) for rows in activated])
    mlp_norm_out, mlp_post = layer_norm(raw_mlp, gains[3], biases[3])
    layer_out = move_tokens((hidden_res + mlp_norm_out).astype(jnp.bfloat16))
    mlp_squares = jnp.sum(raw_mlp * raw_mlp * local_valid)

    upstream = cotangent_rows.astype(jnp.float32) * local_valid
    grad_raw_mlp, gain_three, bias_three = norm_backward(upstream, mlp_post, gains[3])
    grad_mlp_rows = gather_rows(grad_raw_mlp.astype(jnp.bfloat16))
    grad_up = [
        jax.vjp(gelu_tanh, values)[1](project(rows, down_full))[0].astype(jnp.bfloat16)
        for values, rows in zip(up_values, grad_mlp_rows)
    ]
    grad_mlp_in = sum_rows(*[project_back(rows, up_full) for rows in grad_up])
    grad_up_weight = reduce_weight(mlp_rows, grad_up, place, up_bits)
    grad_down_weight = reduce_weight(grad_mlp_rows, activated, place, down_bits)
    grad_hidden_part, gain_two, bias_two = norm_backward(grad_mlp_in, mlp_norm, gains[2])
    grad_hidden = upstream + grad_hidden_part
    grad_raw_attn, gain_one, bias_one = norm_backward(grad_hidden, attn_post, gains[1])
    grad_attn_rows = gather_rows(grad_raw_attn.astype(jnp.bfloat16))
    grad_attended = [project(rows, out_full).astype(jnp.bfloat16) for rows in grad_attn_rows]
    grad_out_weight = reduce_weight(grad_attn_rows, attended, place, down_bits)
    grad_queries, grad_keys, grad_values = attend_backward(
        chunks,
        query_rot,
        key_rot,
        value_rows,
        grad_attended,
        attended,
        log_totals,
        key_segments,
        query_segments,
    )
    grad_qkv = [
        jnp.concatenate(
            [turned(dq, table, -1.0, jnp.bfloat16), turned(dk, table, -1.0, jnp.bfloat16), dv],
            axis=1,
        )
        for dq, dk, dv, table in zip(grad_queries, grad_keys, grad_values, tables)
    ]
    grad_qkv_weight = reduce_weight(attn_rows, grad_qkv, place, up_bits)
    grad_attn_in = sum_rows(*[project_back(rows, qkv_full) for rows in grad_qkv])
    grad_input_part, gain_zero, bias_zero = norm_backward(grad_attn_in, attn_norm, gains[0])
    grad_input = move_tokens((grad_hidden + grad_input_part).astype(jnp.bfloat16))
    stats = jnp.stack([input_squares, attn_squares, mlp_squares, valid_count])
    totals = jnp.stack(
        [
            gain_zero,
            gain_one,
            gain_two,
            gain_three,
            bias_zero,
            bias_one,
            bias_two,
            bias_three,
            jnp.pad(stats, (0, D - 4)),
        ]
    )
    totals = sum_everywhere(totals)
    norm_grads = (
        lax.dynamic_slice(
            totals, (0, (place.dp * lax.axis_size("tensor") + place.tensor) * width), (8, width)
        )
        * grad_scale
    )
    rms_values = jnp.sqrt(totals[8, :3] / (totals[8, 3] * D))
    attn_grads = jnp.split(grad_qkv_weight * grad_scale, 3, axis=1)
    return (
        layer_out,
        grad_input,
        *attn_grads,
        grad_out_weight * grad_scale,
        grad_up_weight * grad_scale,
        grad_down_weight * grad_scale,
        norm_grads[:4],
        norm_grads[4:],
        rms_values,
    )


def solution(mesh):
    in_specs = (
        P(("dp", "tensor"), None),
        P("dp"),
        P("dp"),
        P("dp", "tensor"),
        P("dp", "tensor"),
        P("dp", "tensor"),
        P("dp", "tensor"),
        P("dp", "tensor"),
        P("dp", "tensor"),
        P(None, ("dp", "tensor")),
        P(None, ("dp", "tensor")),
        P(("dp", "tensor"), None),
    )
    out_specs = (
        P(("dp", "tensor"), None),
        P(("dp", "tensor"), None),
        P("dp", "tensor"),
        P("dp", "tensor"),
        P("dp", "tensor"),
        P("dp", "tensor"),
        P("dp", "tensor"),
        P("dp", "tensor"),
        P(None, ("dp", "tensor")),
        P(None, ("dp", "tensor")),
        P(),
    )
    return jax.shard_map(
        per_device, mesh=mesh, in_specs=in_specs, out_specs=out_specs, check_vma=False
    )
```

```python
import functools
import math

import jax
import jax.numpy as jnp
from jax import lax
from jax.experimental import pallas as pl
from jax.experimental.pallas import tpu as pltpu
from jax.sharding import PartitionSpec as P

D = 1024
HEAD_DIM = 64
SEQ_LEN = 1024

EPSILON = 1e-05
MASKED = -1e30
ROPE_BASE = 10000.0

CHUNKS = 4

VMEM = pl.BlockSpec(memory_space=pltpu.VMEM)
SMEM = pl.BlockSpec(memory_space=pltpu.SMEM)

AXES = ("dp", "tensor")
Z_LO, Z_HI, CORE = 1, 2, 4
OUTER_BIT = 3
PIECES = (0, 2, 1, 3)


def device_count():
    return lax.axis_size("dp") * lax.axis_size("tensor")


def exchange(values, mask):
    pairs = [(i, i ^ mask) for i in range(device_count())]
    return lax.ppermute(values, AXES, pairs)


def move_tokens(values):
    def target(i):
        core, z_hi = (i >> 2) & 1, (i >> 1) & 1
        return i if core == z_hi else i ^ (Z_HI | CORE)

    return lax.ppermute(values, AXES, [(i, target(i)) for i in range(device_count())])


def sum_everywhere(values):
    bits = device_count().bit_length() - 1
    values = values + exchange(values, CORE)
    masks = [1 << bit for bit in range(bits) if 1 << bit != CORE]
    for first, second in zip(masks[::2], masks[1::2]):
        values = (values + exchange(values, first)) + (
            exchange(values, second) + exchange(values, first | second)
        )
    if len(masks) % 2:
        values = values + exchange(values, masks[-1])
    return values


def after(values, earlier):
    return lax.optimization_barrier((values, earlier))[0]


def gather_rows(own):
    across = exchange(own, Z_LO)
    return (own, exchange(own, CORE)), (across, exchange(across, CORE))


def sum_rows(near, far):
    across, both = far
    far_sum = across + exchange(both, CORE).astype(jnp.float32)
    far_sum = exchange(far_sum.astype(jnp.bfloat16), Z_LO)
    return near[0], exchange(near[1], CORE), far_sum


class Place:
    def __init__(self):
        self.dp = lax.axis_index("dp")
        self.tensor = lax.axis_index("tensor")
        self.core = self.dp % 2
        self.outer = self.dp // 2
        self.z_lo = self.tensor % 2
        self.z_hi = self.tensor // 2
        self.chunk = 2 * self.core + self.z_lo
        self.at_home = self.core == self.z_hi
        self.outer_bits = (lax.axis_size("dp") // 2).bit_length() - 1


def pick(values, axis, index):
    return lax.dynamic_index_in_dim(values, index, axis, keepdims=False)


def outer(bit):
    return 1 << (OUTER_BIT + bit)


def gather_weight(block, other, place, splits):
    keep = jnp.where(place.at_home, block, other)
    got = exchange(jnp.where(place.at_home, other, block), CORE)
    rows = block.shape[0]
    pair = jnp.where(
        place.core == 0, jnp.concatenate([keep, got]), jnp.concatenate([got, keep])
    )
    pieces = [(0, 0, pair)]
    if place.outer_bits >= 2:
        first, second = exchange(pair, outer(0)), exchange(pair, outer(1))
        pieces += [
            (1, 0, first),
            (2, 0, second),
            (3, 0, exchange(first[:rows], outer(1))),
            (3, rows, exchange(second[rows:], outer(0))),
        ]
        bits = range(2, place.outer_bits)
    else:
        bits = range(place.outer_bits)
    for bit in bits:
        pieces += [
            (label | (1 << bit), start, exchange(piece, outer(bit)))
            for label, start, piece in pieces
        ]
    return assemble(place, pieces, 2 * rows, splits)


def assemble_kernel(layout, rows, splits, outer_ref, *refs):
    sources, targets = refs[: len(layout)], refs[len(layout) :]
    for (label, start), source in zip(layout, sources):
        at = pl.multiple_of((outer_ref[0] ^ label) * rows + start, 16)
        left = 0
        for target, width in zip(targets, splits):
            target[pl.ds(at, source.shape[0]), :] = source[:, left : left + width]
            left += width


def assemble(place, pieces, rows, splits):
    layout = tuple((label, start) for label, start, _ in pieces)
    total = rows << place.outer_bits
    return pl.pallas_call(
        functools.partial(assemble_kernel, layout, rows, splits),
        out_shape=[jax.ShapeDtypeStruct((total, width), jnp.bfloat16) for width in splits],
        in_specs=[SMEM] + [VMEM] * len(pieces),
        out_specs=[VMEM] * len(splits),
        cost_estimate=pl.CostEstimate(
            flops=0, bytes_accessed=4 * total * sum(splits), transcendentals=0
        ),
        name="assemble",
    )(place.outer[None].astype(jnp.int32), *[piece for _, _, piece in pieces])


def weight_kernel(order_ref, *refs):
    lefts, (near, far, x1, y1, rest, turned) = refs[:4], refs[4:]
    step = pl.program_id(0)
    size = lefts[0].shape[0]
    for i, left in enumerate(lefts):
        turned[:, i * size : (i + 1) * size] = left[...].T
    total = dot_nn(turned[:, : 2 * size], near[...]) + dot_nn(turned[:, 2 * size :], far[...])

    @pl.when(step < 2)
    def _():
        x1[0] = total.astype(jnp.bfloat16)

    @pl.when((step >= 2) & (step < 4))
    def _():
        y1[0] = total.astype(jnp.bfloat16)

    @pl.when(step >= 4)
    def _():
        rest[0] = total


BLOCKS = ((3, 0), (1, 0), (3, 1), (2, 1), (1, 1), (2, 0), (0, 0), (0, 1))


def weight_blocks(lefts, rights, place):
    size, width = lefts[0].shape[0], rights[0].shape[1]
    half = lefts[0].shape[1] // 8
    order = jnp.stack([(place.outer ^ label) * 2 + part for label, part in BLOCKS])

    def left_spec():
        return pl.BlockSpec((size, half), lambda b, order: (0, order[b]))

    def right_spec():
        return pl.BlockSpec((2 * size, width), lambda b, order: (0, 0))

    x1, y1, rest = pl.pallas_call(
        weight_kernel,
        out_shape=(
            jax.ShapeDtypeStruct((2, half, width), jnp.bfloat16),
            jax.ShapeDtypeStruct((2, half, width), jnp.bfloat16),
            jax.ShapeDtypeStruct((4, half, width), jnp.float32),
        ),
        grid_spec=pltpu.PrefetchScalarGridSpec(
            num_scalar_prefetch=1,
            grid=(8,),
            in_specs=[left_spec() for _ in range(4)] + [right_spec(), right_spec()],
            out_specs=[
                pl.BlockSpec((1, half, width), lambda b, order: (jnp.clip(b, 0, 1), 0, 0)),
                pl.BlockSpec((1, half, width), lambda b, order: (jnp.clip(b - 2, 0, 1), 0, 0)),
                pl.BlockSpec((1, half, width), lambda b, order: (jnp.clip(b - 4, 0, 3), 0, 0)),
            ],
            scratch_shapes=[pltpu.VMEM((half, 4 * size), jnp.bfloat16)],
        ),
        cost_estimate=pl.CostEstimate(
            flops=64 * half * size * width,
            bytes_accessed=16 * size * (4 * half + width) + 24 * half * width,
            transcendentals=0,
        ),
        name="weight_blocks",
    )(order.astype(jnp.int32), *lefts, *rights)
    return x1, y1, rest


def plain_blocks(lefts, rights, place):
    size = lefts[0].shape[0]
    total = 0.0
    for i, left in enumerate(lefts):
        right = rights[i // 2][(i % 2) * size : (i % 2 + 1) * size]
        total = total + outer_sum(left, right)
    count = 1 << place.outer_bits
    total = total.reshape(count, -1, total.shape[-1])
    total = jnp.stack([pick(total, 0, place.outer ^ label) for label in range(count)])
    for bit in range(place.outer_bits - 1, 1, -1):
        low, high = jnp.split(total, 2)
        total = low + exchange(high.astype(jnp.bfloat16), outer(bit)).astype(jnp.float32)
    total = total.reshape(4, 2, -1, total.shape[-1])
    total = jnp.stack([total[label, part] for label, part in BLOCKS])
    return total[:2].astype(jnp.bfloat16), total[2:4].astype(jnp.bfloat16), total[4:]


def reduce_weight(lefts, rights, place):
    make = weight_blocks if place.outer_bits == 2 else plain_blocks
    x1, y1, rest = make(lefts, rights, place)
    x1, y1 = exchange(x1, outer(0)).astype(jnp.float32), exchange(y1, outer(1)).astype(jnp.float32)
    x2 = exchange((rest[0] + y1[0]).astype(jnp.bfloat16), outer(0)).astype(jnp.float32)
    y2 = exchange((rest[1] + x1[0]).astype(jnp.bfloat16), outer(1)).astype(jnp.float32)
    upper = rest[2] + x1[1] + y2
    lower = rest[3] + y1[1] + x2
    keep = jnp.where(place.core == 0, upper, lower)
    got = exchange(jnp.where(place.core == 0, lower, upper).astype(jnp.bfloat16), CORE)
    got = got.astype(jnp.float32)
    sent = jnp.where(place.at_home, got, keep).astype(jnp.bfloat16)
    return jnp.where(place.at_home, keep, got) + exchange(sent, Z_HI).astype(jnp.float32)


def rotary_tables(position_rows):
    half_size = HEAD_DIM // 2
    inv_freqs = jnp.exp(
        jnp.arange(half_size, dtype=jnp.float32) * (-2.0 * math.log(ROPE_BASE) / HEAD_DIM)
    )
    angles = position_rows.astype(jnp.float32)[:, None] * inv_freqs[None, :]
    cosines, sines = jnp.cos(angles), jnp.sin(angles)
    return (
        jnp.concatenate([cosines] * 4, axis=1),
        jnp.concatenate([-sines, sines, -sines, sines], axis=1),
    )


def rotate(values, cosines, sines):
    half = HEAD_DIM // 2
    lanes = lax.broadcasted_iota(jnp.int32, values.shape, 1) % HEAD_DIM
    other = jnp.where(
        lanes < half,
        pltpu.roll(values, values.shape[1] - half, 1),
        pltpu.roll(values, half, 1),
    )
    wide = values.shape[1] // cosines.shape[1]
    return values * jnp.concatenate([cosines] * wide, axis=1) + other * jnp.concatenate(
        [sines] * wide, axis=1
    )


def dot_nt(left, right):
    return lax.dot_general(
        left, right, (((1,), (1,)), ((), ())), preferred_element_type=jnp.float32
    )


def dot_nn(left, right):
    return jnp.dot(left, right, preferred_element_type=jnp.float32)


def head_lanes(values, head):
    lanes = lax.broadcasted_iota(jnp.int32, values.shape, 1) // HEAD_DIM
    return jnp.where(lanes == head, values, jnp.zeros_like(values))


def fill_bias(bias_ref, key_segments, query_segments, j, size):
    query_row = query_segments[:, j * size : (j + 1) * size]
    for i in range(j + 1):
        same = key_segments[i * size : (i + 1) * size, :1] == query_row
        if i == j:
            key_at = lax.broadcasted_iota(jnp.int32, (size, size), 0)
            query_at = lax.broadcasted_iota(jnp.int32, (size, size), 1)
            same = same & (key_at <= query_at)
        bias_ref[i] = jnp.where(same, 0.0, MASKED)


def in_order(chunks, near_ref, far_ref, held_ref):
    size = near_ref.shape[0] // 2
    for s in range(CHUNKS):
        source = near_ref if s < 2 else far_ref
        held_ref[pl.ds(pl.multiple_of(chunks[s] * size, size), size), :] = source[
            (s % 2) * size : (s % 2 + 1) * size, :
        ]


def in_pieces(chunks, held_ref, near_ref, far_ref):
    size = near_ref.shape[0] // 2
    for s in range(CHUNKS):
        target = near_ref if s < 2 else far_ref
        target[(s % 2) * size : (s % 2 + 1) * size, :] = held_ref[
            pl.ds(pl.multiple_of(chunks[s] * size, size), size), :
        ].astype(target.dtype)


def attend_kernel(
    chunks, qn, qf, kn, kf, vn, vf, key_segments, query_segments,
    out_near, out_far, lse_ref, q_all, k_all, v_all, vt_ref, ot_ref, out_all, bias_ref,
):
    in_order(chunks, qn, qf, q_all)
    in_order(chunks, kn, kf, k_all)
    in_order(chunks, vn, vf, v_all)
    size = q_all.shape[0] // CHUNKS
    heads = q_all.shape[1] // HEAD_DIM
    lse_ref[...] = jnp.zeros_like(lse_ref)
    for i in range(CHUNKS):
        here = slice(i * size, (i + 1) * size)
        vt_ref[:, here] = v_all[here, :].T
    for j in range(CHUNKS):
        fill_bias(bias_ref, key_segments, query_segments, j, size)
        mine = slice(j * size, (j + 1) * size)

        def one_head(head):
            query = head_lanes(q_all[mine, :], head) * jnp.bfloat16(HEAD_DIM**-0.5)
            features = slice(head * HEAD_DIM, (head + 1) * HEAD_DIM)
            row = slice(head, head + 1)
            scores = [
                dot_nt(k_all[i * size : (i + 1) * size, :], query) + bias_ref[i]
                for i in range(j + 1)
            ]
            top = functools.reduce(
                jnp.maximum, [jnp.max(s, axis=0, keepdims=True) for s in scores]
            )
            expo = [jnp.exp(s - top) for s in scores]
            total = sum(jnp.sum(e, axis=0, keepdims=True) for e in expo)
            mixed = sum(
                dot_nn(vt_ref[features, i * size : (i + 1) * size], expo[i].astype(jnp.bfloat16))
                for i in range(j + 1)
            )
            ot_ref[features, :] = mixed * (1.0 / total)
            lse_ref[row, mine] = top + jnp.log(total)

        for head in range(heads):
            one_head(head)
        out_all[mine, :] = ot_ref[...].T.astype(out_all.dtype)
    in_pieces(chunks, out_all, out_near, out_far)


def attend_back_kernel(
    chunks, qn, qf, kn, kf, vn, vf, don, dof, on, of, lse_ref, key_segments, query_segments,
    cos_near, cos_far, sin_near, sin_far, near_ref, far_ref,
    q_all, k_all, v_all, do_all, o_all, kt_ref, dqt_ref, delta_ref, bias_ref, dq_sum, dk_sum, dv_sum,
):
    for near, far, held in ((qn, qf, q_all), (kn, kf, k_all), (vn, vf, v_all), (don, dof, do_all), (on, of, o_all)):
        in_order(chunks, near, far, held)
    size = q_all.shape[0] // CHUNKS
    heads = q_all.shape[1] // HEAD_DIM
    for i in range(CHUNKS):
        here = slice(i * size, (i + 1) * size)
        kt_ref[:, here] = k_all[here, :].T
    dk_sum[...] = jnp.zeros_like(dk_sum)
    dv_sum[...] = jnp.zeros_like(dv_sum)
    for j in range(CHUNKS):
        fill_bias(bias_ref, key_segments, query_segments, j, size)
        mine = slice(j * size, (j + 1) * size)
        delta_ref[...] = (
            do_all[mine, :].astype(jnp.float32) * o_all[mine, :].astype(jnp.float32)
        ).T

        def one_head(head):
            query = head_lanes(q_all[mine, :], head) * jnp.bfloat16(HEAD_DIM**-0.5)
            upstream = head_lanes(do_all[mine, :], head)
            features = slice(head * HEAD_DIM, (head + 1) * HEAD_DIM)
            row = slice(head, head + 1)
            delta = jnp.sum(delta_ref[features, :], axis=0, keepdims=True)
            lse = lse_ref[row, mine]
            dqt = jnp.zeros((HEAD_DIM, size), jnp.float32)
            for i in range(j + 1):
                here = slice(i * size, (i + 1) * size)
                probs = jnp.exp(dot_nt(k_all[here, :], query) + bias_ref[i] - lse)
                dprobs = dot_nt(v_all[here, :], upstream)
                dscores = (probs * (dprobs - delta)).astype(jnp.bfloat16)
                dv_sum[here, :] += dot_nn(probs.astype(jnp.bfloat16), upstream)
                dk_sum[here, :] += dot_nn(dscores, query)
                dqt += dot_nn(kt_ref[features, here], dscores)
            dqt_ref[features, :] = dqt

        for head in range(heads):
            one_head(head)
        dq_sum[mine, :] = dqt_ref[...].T * HEAD_DIM**-0.5
    width = q_all.shape[1]
    for s in range(CHUNKS):
        target, cosines, sines = (
            (near_ref, cos_near, sin_near) if s < 2 else (far_ref, cos_far, sin_far)
        )
        there = slice((s % 2) * size, (s % 2 + 1) * size)
        here = pl.ds(pl.multiple_of(chunks[s] * size, size), size)
        for n, held in enumerate((dq_sum, dk_sum)):
            target[there, n * width : (n + 1) * width] = rotate(
                held[here, :], cosines[there, :], -sines[there, :]
            ).astype(jnp.bfloat16)
        target[there, 2 * width :] = dv_sum[here, :].astype(jnp.bfloat16)


def halves(tokens, width, kind):
    return [jax.ShapeDtypeStruct((tokens // 2, width), kind)] * 2


def attend_forward(chunks, queries, keys_in, values_in, key_segments, query_segments):
    tokens, width = query_segments.shape[1], queries[0].shape[1]
    size = tokens // CHUNKS
    near, far, lse = pl.pallas_call(
        attend_kernel,
        out_shape=(
            *halves(tokens, width, jnp.bfloat16),
            jax.ShapeDtypeStruct((8, tokens), jnp.float32),
        ),
        in_specs=[SMEM] + [VMEM] * 8,
        out_specs=(VMEM,) * 3,
        scratch_shapes=[pltpu.VMEM((tokens, width), jnp.bfloat16)] * 3
        + [
            pltpu.VMEM((width, tokens), jnp.bfloat16),
            pltpu.VMEM((width, size), jnp.float32),
            pltpu.VMEM((tokens, width), jnp.bfloat16),
            pltpu.VMEM((CHUNKS, size, size), jnp.float32),
        ],
        cost_estimate=pl.CostEstimate(
            flops=4 * tokens * tokens * width,
            bytes_accessed=8 * tokens * width,
            transcendentals=4 * tokens * tokens,
        ),
        name="attend_forward",
    )(chunks, *queries, *keys_in, *values_in, key_segments, query_segments)
    return (near, far), lse


def attend_backward(
    chunks, queries, keys_in, values_in, grad_attended, attended, lse, key_segments,
    query_segments, cosines, sines,
):
    tokens, width = query_segments.shape[1], queries[0].shape[1]
    size = tokens // CHUNKS
    return pl.pallas_call(
        attend_back_kernel,
        out_shape=halves(tokens, 3 * width, jnp.bfloat16),
        in_specs=[SMEM] + [VMEM] * 17,
        out_specs=[VMEM] * 2,
        scratch_shapes=[pltpu.VMEM((tokens, width), jnp.bfloat16)] * 5
        + [
            pltpu.VMEM((width, tokens), jnp.bfloat16),
            pltpu.VMEM((width, size), jnp.float32),
            pltpu.VMEM((width, size), jnp.float32),
            pltpu.VMEM((CHUNKS, size, size), jnp.float32),
        ]
        + [pltpu.VMEM((tokens, width), jnp.float32)] * 3,
        cost_estimate=pl.CostEstimate(
            flops=10 * tokens * tokens * width,
            bytes_accessed=16 * tokens * width,
            transcendentals=4 * tokens * tokens,
        ),
        name="attend_backward",
    )(
        chunks, *queries, *keys_in, *values_in, *grad_attended, *attended, lse,
        key_segments, query_segments, *cosines, *sines,
    )


def outer_sum(left, right):
    return lax.dot_general(
        left, right, (((0,), (0,)), ((), ())), preferred_element_type=jnp.float32
    )


def call(kernel, name, outs, *args, scratch=(), flops=0, transcendentals=0):
    moved = sum(a.size * a.dtype.itemsize for a in args)
    moved += sum(math.prod(shape) * jnp.dtype(kind).itemsize for shape, kind in outs)
    return pl.pallas_call(
        kernel,
        out_shape=[jax.ShapeDtypeStruct(shape, kind) for shape, kind in outs],
        in_specs=[VMEM] * len(args),
        out_specs=[VMEM] * len(outs),
        scratch_shapes=scratch,
        cost_estimate=pl.CostEstimate(
            flops=flops, bytes_accessed=moved, transcendentals=transcendentals
        ),
        name=name,
    )(*args)


def qkv_kernel(first, second, weight, cosines, sines, q_ref, k_ref, v_ref):
    size, width = first.shape[0], q_ref.shape[1]
    for p, rows in enumerate((first, second)):
        here = slice(p * size, (p + 1) * size)
        for n, target in enumerate((q_ref, k_ref, v_ref)):
            values = dot_nn(rows[...], weight[:, n * width : (n + 1) * width])
            if n < 2:
                values = rotate(values, cosines[here, :], sines[here, :])
            target[here, :] = values.astype(jnp.bfloat16)


def qkv_rows(pieces, weight, cosines, sines):
    rows, width = 2 * pieces[0].shape[0], weight.shape[1] // 3
    return call(
        qkv_kernel,
        "qkv_rows",
        [((rows, width), jnp.bfloat16)] * 3,
        *pieces,
        weight,
        cosines,
        sines,
        flops=2 * rows * weight.size,
    )


TILE = 256


def tiles(total, body):
    @pl.loop(0, total // TILE)
    def _(n):
        body(pl.ds(pl.multiple_of(n * TILE, TILE), TILE))


def back_kernel(rows, weight, first, second):
    size = first.shape[0]

    def tile(columns):
        values = dot_nt(rows[...], weight[columns, :])
        first[:, columns] = values[:size]
        second[:, columns] = values[size:].astype(jnp.bfloat16)

    tiles(weight.shape[0], tile)


def project_back(rows, weight):
    size = rows.shape[0] // 2
    return call(
        back_kernel,
        "project_back",
        [((size, weight.shape[0]), jnp.float32), ((size, weight.shape[0]), jnp.bfloat16)],
        rows,
        weight,
        flops=2 * rows.shape[0] * weight.size,
    )


ROOT = math.sqrt(2.0 / math.pi)
CUBE = 0.044715


def up_kernel(first, second, weight, act_ref, slope_ref):
    size = first.shape[0]

    def tile(columns):
        for p, rows in enumerate((first, second)):
            here = slice(p * size, (p + 1) * size)
            up = dot_nn(rows[...], weight[:, columns])
            square = up * up
            bent = jnp.tanh(up * (ROOT + (ROOT * CUBE) * square))
            half = 0.5 + 0.5 * bent
            act_ref[here, columns] = (up * half).astype(jnp.bfloat16)
            slope = half + (half - half * bent) * up * (ROOT + (3.0 * ROOT * CUBE) * square)
            slope_ref[here, columns] = slope.astype(jnp.bfloat16)

    tiles(weight.shape[1], tile)


def up_rows(pieces, weight):
    shape = (2 * pieces[0].shape[0], weight.shape[1])
    return call(
        up_kernel,
        "up_rows",
        [(shape, jnp.bfloat16)] * 2,
        *pieces,
        weight,
        flops=2 * shape[0] * weight.size,
        transcendentals=shape[0] * shape[1],
    )


def up_back_kernel(first, second, weight, slope_ref, out_ref):
    size = first.shape[0]

    def tile(columns):
        for p, rows in enumerate((first, second)):
            here = slice(p * size, (p + 1) * size)
            grad = dot_nn(rows[...], weight[:, columns])
            grad = grad * slope_ref[here, columns].astype(jnp.float32)
            out_ref[here, columns] = grad.astype(jnp.bfloat16)

    tiles(weight.shape[1], tile)


def up_back(pieces, weight, slope):
    return call(
        up_back_kernel,
        "up_back",
        [(slope.shape, jnp.bfloat16)],
        *pieces,
        weight,
        slope,
        flops=2 * slope.shape[0] * weight.size,
    )[0]


def plain_kernel(first, second, weight, out_ref):
    size = first.shape[0]
    for p, rows in enumerate((first, second)):
        out_ref[p * size : (p + 1) * size, :] = dot_nn(rows[...], weight[...]).astype(jnp.bfloat16)


def project(pieces, weight):
    shape = (2 * pieces[0].shape[0], weight.shape[1])
    return call(
        plain_kernel,
        "project",
        [(shape, jnp.bfloat16)],
        *pieces,
        weight,
        flops=2 * shape[0] * weight.size,
    )[0]


STEP = 32


def row_steps(total, body):
    @pl.loop(0, total // STEP)
    def _(n):
        body(pl.ds(pl.multiple_of(n * STEP, STEP), STEP))


def normed(values):
    centred = values - jnp.mean(values, axis=-1, keepdims=True)
    variance = jnp.mean(centred * centred, axis=-1, keepdims=True)
    inv_std = lax.rsqrt(variance + EPSILON)
    return centred * inv_std, inv_std


def norm_back(upstream, hat, inv_std, gain):
    scaled = upstream * gain
    first_mean = jnp.mean(scaled, axis=-1, keepdims=True)
    cross_mean = jnp.mean(scaled * hat, axis=-1, keepdims=True)
    return inv_std * (scaled - first_mean - hat * cross_mean)


def add_rows(sum_ref, index, values):
    sum_ref[index] += functools.reduce(
        jnp.add, [values[i : i + 8, :] for i in range(0, values.shape[0], 8)]
    )


def whole(own, beside, far, rows):
    return own[rows, :] + beside[rows, :].astype(jnp.float32) + far[rows, :].astype(jnp.float32)


def start_kernel(residual, params, valid, a_ref, sums, held):
    held[...] = jnp.zeros_like(held)

    def step(rows):
        values = residual[rows, :].astype(jnp.float32)
        hat, _ = normed(values)
        a_ref[rows, :] = (hat * params[0:1, :] + params[4:5, :]).astype(jnp.bfloat16)
        add_rows(held, 0, values * values * valid[rows, :1])

    row_steps(residual.shape[0], step)
    sums[...] = jnp.sum(held[...], axis=1)


def middle_kernel(own, beside, far, residual, params, valid, raw_ref, h_ref, b_ref, sums, held):
    held[...] = jnp.zeros_like(held)

    def step(rows):
        raw = whole(own, beside, far, rows)
        raw_ref[rows, :] = raw
        hat, _ = normed(raw)
        hidden = residual[rows, :].astype(jnp.float32) + (hat * params[1:2, :] + params[5:6, :])
        h_ref[rows, :] = hidden
        hat, _ = normed(hidden)
        b_ref[rows, :] = (hat * params[2:3, :] + params[6:7, :]).astype(jnp.bfloat16)
        add_rows(held, 0, raw * raw * valid[rows, :1])

    row_steps(residual.shape[0], step)
    sums[...] = jnp.sum(held[...], axis=1)


def top_kernel(
    own, beside, far, hidden, cotangent, params, valid, out_ref, grad_ref, sums, held
):
    held[...] = jnp.zeros_like(held)

    def step(rows):
        raw = whole(own, beside, far, rows)
        hat, inv_std = normed(raw)
        out = hidden[rows, :] + (hat * params[3:4, :] + params[7:8, :])
        out_ref[rows, :] = out.astype(jnp.bfloat16)
        upstream = cotangent[rows, :].astype(jnp.float32) * valid[rows, :1]
        grad = norm_back(upstream, hat, inv_std, params[3:4, :])
        grad_ref[rows, :] = grad.astype(jnp.bfloat16)
        add_rows(held, 0, raw * raw * valid[rows, :1])
        add_rows(held, 1, upstream * hat)
        add_rows(held, 2, upstream)

    row_steps(hidden.shape[0], step)
    sums[...] = jnp.sum(held[...], axis=1)


def middle_back_kernel(
    own, beside, far, hidden, raw_attn, cotangent, params, valid, dh_ref, grad_ref, sums, held
):
    held[...] = jnp.zeros_like(held)

    def step(rows):
        grad_b = whole(own, beside, far, rows)
        hat, inv_std = normed(hidden[rows, :])
        add_rows(held, 0, grad_b * hat)
        add_rows(held, 1, grad_b)
        upstream = cotangent[rows, :].astype(jnp.float32) * valid[rows, :1]
        grad_h = upstream + norm_back(grad_b, hat, inv_std, params[2:3, :])
        dh_ref[rows, :] = grad_h
        hat, inv_std = normed(raw_attn[rows, :])
        add_rows(held, 2, grad_h * hat)
        add_rows(held, 3, grad_h)
        grad = norm_back(grad_h, hat, inv_std, params[1:2, :])
        grad_ref[rows, :] = grad.astype(jnp.bfloat16)

    row_steps(hidden.shape[0], step)
    sums[...] = jnp.sum(held[...], axis=1)


def end_kernel(own, beside, far, residual, grad_h, params, out_ref, sums, held):
    held[...] = jnp.zeros_like(held)

    def step(rows):
        grad_a = whole(own, beside, far, rows)
        hat, inv_std = normed(residual[rows, :].astype(jnp.float32))
        add_rows(held, 0, grad_a * hat)
        add_rows(held, 1, grad_a)
        grad = grad_h[rows, :] + norm_back(grad_a, hat, inv_std, params[0:1, :])
        out_ref[rows, :] = grad.astype(jnp.bfloat16)

    row_steps(residual.shape[0], step)
    sums[...] = jnp.sum(held[...], axis=1)


def on_rows(kernel, name, kinds, count, *args):
    shape = args[0].shape
    return call(
        kernel,
        name,
        [(shape, kind) for kind in kinds] + [((count, shape[1]), jnp.float32)],
        *args,
        scratch=[pltpu.VMEM((count, 8, shape[1]), jnp.float32)],
        flops=40 * shape[0] * shape[1],
    )


def per_device(
    residual_in,
    segments,
    positions,
    query_weight,
    key_weight,
    value_weight,
    out_weight,
    up_weight,
    down_weight,
    norm_gains,
    norm_biases,
    cotangent,
):
    place = Place()
    local_rows = residual_in.shape[0]
    group_rows = segments.shape[0]
    grad_scale = 1.0 / math.sqrt(group_rows * lax.axis_size("dp"))
    bf16, f32 = jnp.bfloat16, jnp.float32

    qkv_block = jnp.concatenate([query_weight, key_weight, value_weight], axis=1)
    qkv_other = exchange(qkv_block, Z_HI)
    residual = move_tokens(residual_in)
    numbers = jnp.stack([segments, positions])
    numbers = jnp.where(place.at_home, numbers, exchange(numbers, CORE))
    query_segments = numbers[:1]
    key_segments = jnp.broadcast_to(numbers[0][:, None], (group_rows, 128))
    numbers = numbers.reshape(2, 4, local_rows)
    numbers = jnp.stack([pick(numbers, 1, place.chunk ^ p) for p in PIECES], axis=1)
    chunks = jnp.stack([place.chunk ^ p for p in PIECES]).astype(jnp.int32)
    valid = (numbers[0, 0] >= 0).astype(f32)[:, None]
    valid_count = jnp.sum(valid)
    valid = jnp.broadcast_to(valid, (local_rows, 128))
    cosines, sines = rotary_tables(numbers[1].reshape(-1))
    cosines, sines = jnp.split(cosines, 2), jnp.split(sines, 2)

    params = jnp.concatenate([norm_gains, norm_biases])
    width = params.shape[1]
    at = (place.dp * lax.axis_size("tensor") + place.tensor) * width
    params = lax.dynamic_update_slice(jnp.zeros((params.shape[0], D), f32), params, (0, at))
    params = sum_everywhere(params)

    (qkv_full,) = gather_weight(qkv_block, qkv_other, place, (qkv_block.shape[1],))
    later_block = jnp.concatenate([out_weight, up_weight], axis=1)
    later_block = after(later_block, (qkv_other, residual))
    later_other = exchange(later_block, Z_HI)
    out_full, up_full = gather_weight(
        later_block, later_other, place, (out_weight.shape[1], up_weight.shape[1])
    )
    down_block = after(down_weight, later_other)
    down_other = exchange(down_block, Z_HI)
    (down_full,) = gather_weight(down_block, down_other, place, (down_weight.shape[1],))
    cotangent_rows = move_tokens(after(cotangent, down_other))

    attn_in, input_sums = on_rows(
        start_kernel, "start", [bf16], 1, residual, params, valid
    )
    attn_rows = gather_rows(attn_in)
    queries, keys, values = zip(
        *[
            qkv_rows(rows, qkv_full, cos_rows, sin_rows)
            for rows, cos_rows, sin_rows in zip(attn_rows, cosines, sines)
        ]
    )
    attended, log_totals = attend_forward(
        chunks, queries, keys, values, key_segments, query_segments
    )
    raw_attn, hidden, mlp_in, attn_sums = on_rows(
        middle_kernel,
        "middle",
        [f32, f32, bf16],
        1,
        *sum_rows(*[project_back(rows, out_full) for rows in attended]),
        residual,
        params,
        valid,
    )
    mlp_rows = gather_rows(mlp_in)
    activated, slopes = zip(*[up_rows(rows, up_full) for rows in mlp_rows])
    layer_out, grad_raw_mlp, top_sums = on_rows(
        top_kernel,
        "top",
        [bf16, bf16],
        3,
        *sum_rows(*[project_back(rows, down_full) for rows in activated]),
        hidden,
        cotangent_rows,
        params,
        valid,
    )
    layer_out = move_tokens(layer_out)
    grad_mlp_rows = gather_rows(grad_raw_mlp)
    grad_up = [up_back(rows, down_full, slope) for rows, slope in zip(grad_mlp_rows, slopes)]
    grad_b = sum_rows(*[project_back(rows, up_full) for rows in grad_up])
    grad_up_weight = reduce_weight(sum(mlp_rows, ()), grad_up, place)
    grad_down_weight = reduce_weight(sum(grad_mlp_rows, ()), activated, place)
    grad_hidden, grad_raw_attn, middle_sums = on_rows(
        middle_back_kernel,
        "middle_back",
        [f32, bf16],
        4,
        *grad_b,
        hidden,
        raw_attn,
        cotangent_rows,
        params,
        valid,
    )
    grad_attn_rows = gather_rows(grad_raw_attn)
    grad_attended = [project(rows, out_full) for rows in grad_attn_rows]
    grad_out_weight = reduce_weight(sum(grad_attn_rows, ()), attended, place)
    grad_qkv = attend_backward(
        chunks,
        queries,
        keys,
        values,
        grad_attended,
        attended,
        log_totals,
        key_segments,
        query_segments,
        cosines,
        sines,
    )
    grad_a = sum_rows(*[project_back(rows, qkv_full) for rows in grad_qkv])
    grad_qkv_weight = reduce_weight(sum(attn_rows, ()), grad_qkv, place)
    grad_input, end_sums = on_rows(
        end_kernel, "end", [bf16], 2, *grad_a, residual, grad_hidden, params
    )
    grad_input = move_tokens(grad_input)
    totals = jnp.concatenate(
        [
            end_sums,
            middle_sums,
            top_sums,
            input_sums,
            attn_sums,
            jnp.pad(valid_count[None, None], ((0, 0), (0, D - 1))),
        ]
    )
    totals = sum_everywhere(totals)
    mine = lax.dynamic_slice(totals, (0, at), (totals.shape[0], width)) * grad_scale
    gain_grads = jnp.stack([mine[0], mine[4], mine[2], mine[7]])
    bias_grads = jnp.stack([mine[1], mine[5], mine[3], mine[8]])
    squares = jnp.sum(totals, axis=1)
    rms_values = jnp.sqrt(
        jnp.stack([squares[9], squares[10], squares[6]]) / (squares[11] * D)
    )
    return (
        layer_out,
        grad_input,
        *jnp.split(grad_qkv_weight * grad_scale, 3, axis=1),
        grad_out_weight * grad_scale,
        grad_up_weight * grad_scale,
        grad_down_weight * grad_scale,
        gain_grads,
        bias_grads,
        rms_values,
    )


def solution(mesh):
    in_specs = (
        P(("dp", "tensor"), None),
        P("dp"),
        P("dp"),
        P("dp", "tensor"),
        P("dp", "tensor"),
        P("dp", "tensor"),
        P("dp", "tensor"),
        P("dp", "tensor"),
        P("dp", "tensor"),
        P(None, ("dp", "tensor")),
        P(None, ("dp", "tensor")),
        P(("dp", "tensor"), None),
    )
    out_specs = (
        P(("dp", "tensor"), None),
        P(("dp", "tensor"), None),
        P("dp", "tensor"),
        P("dp", "tensor"),
        P("dp", "tensor"),
        P("dp", "tensor"),
        P("dp", "tensor"),
        P("dp", "tensor"),
        P(None, ("dp", "tensor")),
        P(None, ("dp", "tensor")),
        P(),
    )
    return jax.shard_map(
        per_device, mesh=mesh, in_specs=in_specs, out_specs=out_specs, check_vma=False
    )
```

```python
import functools
import math

import jax
import jax.numpy as jnp
from jax import lax
from jax.experimental import pallas as pl
from jax.experimental.pallas import tpu as pltpu
from jax.sharding import PartitionSpec as P

D = 1024
HEAD_DIM = 64
SEQ_LEN = 1024

EPSILON = 1e-05
MASKED = -1e30
ROPE_BASE = 10000.0

CHUNKS = 4

VMEM = pl.BlockSpec(memory_space=pltpu.VMEM)
SMEM = pl.BlockSpec(memory_space=pltpu.SMEM)

AXES = ("dp", "tensor")
Z_LO, Z_HI, CORE = 1, 2, 4
OUTER_BIT = 3
PIECES = (0, 2, 1, 3)


def device_count():
    return lax.axis_size("dp") * lax.axis_size("tensor")


def exchange(values, mask):
    pairs = [(i, i ^ mask) for i in range(device_count())]
    return lax.ppermute(values, AXES, pairs)


def move_tokens(values):
    def target(i):
        core, z_hi = (i >> 2) & 1, (i >> 1) & 1
        return i if core == z_hi else i ^ (Z_HI | CORE)

    return lax.ppermute(values, AXES, [(i, target(i)) for i in range(device_count())])


def sum_everywhere(values):
    bits = device_count().bit_length() - 1
    values = values + exchange(values, CORE)
    masks = [1 << bit for bit in range(bits) if 1 << bit != CORE]
    for first, second in zip(masks[::2], masks[1::2]):
        values = (values + exchange(values, first)) + (
            exchange(values, second) + exchange(values, first | second)
        )
    if len(masks) % 2:
        values = values + exchange(values, masks[-1])
    return values


def after(values, earlier):
    return lax.optimization_barrier((values, earlier))[0]


def gather_rows(own):
    across = exchange(own, Z_LO)
    return (own, exchange(own, CORE)), (across, exchange(across, CORE))


def sum_rows(near, far):
    across, both = far
    far_sum = across + exchange(both, CORE).astype(jnp.float32)
    far_sum = exchange(far_sum.astype(jnp.bfloat16), Z_LO)
    return near[0], exchange(near[1], CORE), far_sum


class Place:
    def __init__(self):
        self.dp = lax.axis_index("dp")
        self.tensor = lax.axis_index("tensor")
        self.core = self.dp % 2
        self.outer = self.dp // 2
        self.z_lo = self.tensor % 2
        self.z_hi = self.tensor // 2
        self.chunk = 2 * self.core + self.z_lo
        self.at_home = self.core == self.z_hi
        self.outer_bits = (lax.axis_size("dp") // 2).bit_length() - 1


def pick(values, axis, index):
    return lax.dynamic_index_in_dim(values, index, axis, keepdims=False)


def outer(bit):
    return 1 << (OUTER_BIT + bit)


def gather_weight(block, other, place, splits):
    keep = jnp.where(place.at_home, block, other)
    got = exchange(jnp.where(place.at_home, other, block), CORE)
    rows = block.shape[0]
    pair = jnp.where(
        place.core == 0, jnp.concatenate([keep, got]), jnp.concatenate([got, keep])
    )
    pieces = [(0, 0, pair)]
    if place.outer_bits >= 2:
        first, second = exchange(pair, outer(0)), exchange(pair, outer(1))
        pieces += [
            (1, 0, first),
            (2, 0, second),
            (3, 0, exchange(first[:rows], outer(1))),
            (3, rows, exchange(second[rows:], outer(0))),
        ]
        bits = range(2, place.outer_bits)
    else:
        bits = range(place.outer_bits)
    for bit in bits:
        pieces += [
            (label | (1 << bit), start, exchange(piece, outer(bit)))
            for label, start, piece in pieces
        ]
    return assemble(place, pieces, 2 * rows, splits)


def assemble_kernel(layout, rows, splits, outer_ref, *refs):
    sources, targets = refs[: len(layout)], refs[len(layout) :]
    for (label, start), source in zip(layout, sources):
        at = pl.multiple_of((outer_ref[0] ^ label) * rows + start, 16)
        left = 0
        for target, width in zip(targets, splits):
            target[pl.ds(at, source.shape[0]), :] = source[:, left : left + width]
            left += width


def assemble(place, pieces, rows, splits):
    layout = tuple((label, start) for label, start, _ in pieces)
    total = rows << place.outer_bits
    return pl.pallas_call(
        functools.partial(assemble_kernel, layout, rows, splits),
        out_shape=[jax.ShapeDtypeStruct((total, width), jnp.bfloat16) for width in splits],
        in_specs=[SMEM] + [VMEM] * len(pieces),
        out_specs=[VMEM] * len(splits),
        cost_estimate=pl.CostEstimate(
            flops=0, bytes_accessed=4 * total * sum(splits), transcendentals=0
        ),
        compiler_params=grant(4 * total * sum(splits)),
        name="assemble",
    )(place.outer[None].astype(jnp.int32), *[piece for _, _, piece in pieces])


def weight_kernel(order_ref, *refs):
    lefts, (near, far, x1, y1, rest, turned) = refs[:4], refs[4:]
    step = pl.program_id(0)
    size = lefts[0].shape[0]
    for i, left in enumerate(lefts):
        turned[:, i * size : (i + 1) * size] = left[...].T
    total = dot_nn(turned[:, : 2 * size], near[...]) + dot_nn(turned[:, 2 * size :], far[...])

    @pl.when(step < 2)
    def _():
        x1[0] = total.astype(jnp.bfloat16)

    @pl.when((step >= 2) & (step < 4))
    def _():
        y1[0] = total.astype(jnp.bfloat16)

    @pl.when(step >= 4)
    def _():
        rest[0] = total


BLOCKS = ((3, 0), (1, 0), (3, 1), (2, 1), (1, 1), (2, 0), (0, 0), (0, 1))


def weight_blocks(lefts, rights, place):
    size, width = lefts[0].shape[0], rights[0].shape[1]
    half = lefts[0].shape[1] // 8
    order = jnp.stack([(place.outer ^ label) * 2 + part for label, part in BLOCKS])

    def left_spec():
        return pl.BlockSpec((size, half), lambda b, order: (0, order[b]))

    def right_spec():
        return pl.BlockSpec((2 * size, width), lambda b, order: (0, 0))

    x1, y1, rest = pl.pallas_call(
        weight_kernel,
        out_shape=(
            jax.ShapeDtypeStruct((2, half, width), jnp.bfloat16),
            jax.ShapeDtypeStruct((2, half, width), jnp.bfloat16),
            jax.ShapeDtypeStruct((4, half, width), jnp.float32),
        ),
        grid_spec=pltpu.PrefetchScalarGridSpec(
            num_scalar_prefetch=1,
            grid=(8,),
            in_specs=[left_spec() for _ in range(4)] + [right_spec(), right_spec()],
            out_specs=[
                pl.BlockSpec((1, half, width), lambda b, order: (jnp.clip(b, 0, 1), 0, 0)),
                pl.BlockSpec((1, half, width), lambda b, order: (jnp.clip(b - 2, 0, 1), 0, 0)),
                pl.BlockSpec((1, half, width), lambda b, order: (jnp.clip(b - 4, 0, 3), 0, 0)),
            ],
            scratch_shapes=[pltpu.VMEM((half, 4 * size), jnp.bfloat16)],
        ),
        cost_estimate=pl.CostEstimate(
            flops=64 * half * size * width,
            bytes_accessed=16 * size * (4 * half + width) + 24 * half * width,
            transcendentals=0,
        ),
        compiler_params=grant(16 << 20),
        name="weight_blocks",
    )(order.astype(jnp.int32), *lefts, *rights)
    return x1, y1, rest


def plain_blocks(lefts, rights, place):
    size = lefts[0].shape[0]
    total = 0.0
    for i, left in enumerate(lefts):
        right = rights[i // 2][(i % 2) * size : (i % 2 + 1) * size]
        total = total + outer_sum(left, right)
    count = 1 << place.outer_bits
    total = total.reshape(count, -1, total.shape[-1])
    total = jnp.stack([pick(total, 0, place.outer ^ label) for label in range(count)])
    for bit in range(place.outer_bits - 1, 1, -1):
        low, high = jnp.split(total, 2)
        total = low + exchange(high.astype(jnp.bfloat16), outer(bit)).astype(jnp.float32)
    total = total.reshape(4, 2, -1, total.shape[-1])
    total = jnp.stack([total[label, part] for label, part in BLOCKS])
    return total[:2].astype(jnp.bfloat16), total[2:4].astype(jnp.bfloat16), total[4:]


def reduce_weight(lefts, rights, place):
    make = weight_blocks if place.outer_bits == 2 else plain_blocks
    x1, y1, rest = make(lefts, rights, place)
    x1, y1 = exchange(x1, outer(0)).astype(jnp.float32), exchange(y1, outer(1)).astype(jnp.float32)
    x2 = exchange((rest[0] + y1[0]).astype(jnp.bfloat16), outer(0)).astype(jnp.float32)
    y2 = exchange((rest[1] + x1[0]).astype(jnp.bfloat16), outer(1)).astype(jnp.float32)
    upper = rest[2] + x1[1] + y2
    lower = rest[3] + y1[1] + x2
    keep = jnp.where(place.core == 0, upper, lower)
    got = exchange(jnp.where(place.core == 0, lower, upper).astype(jnp.bfloat16), CORE)
    got = got.astype(jnp.float32)
    sent = jnp.where(place.at_home, got, keep).astype(jnp.bfloat16)
    return jnp.where(place.at_home, keep, got) + exchange(sent, Z_HI).astype(jnp.float32)


def rotary_tables(position_rows):
    half_size = HEAD_DIM // 2
    inv_freqs = jnp.exp(
        jnp.arange(half_size, dtype=jnp.float32) * (-2.0 * math.log(ROPE_BASE) / HEAD_DIM)
    )
    angles = position_rows.astype(jnp.float32)[:, None] * inv_freqs[None, :]
    cosines, sines = jnp.cos(angles), jnp.sin(angles)
    return (
        jnp.concatenate([cosines] * 4, axis=1),
        jnp.concatenate([-sines, sines, -sines, sines], axis=1),
    )


def rotate(values, cosines, sines):
    half = HEAD_DIM // 2
    lanes = lax.broadcasted_iota(jnp.int32, values.shape, 1) % HEAD_DIM
    other = jnp.where(
        lanes < half,
        pltpu.roll(values, values.shape[1] - half, 1),
        pltpu.roll(values, half, 1),
    )
    wide = values.shape[1] // cosines.shape[1]
    return values * jnp.concatenate([cosines] * wide, axis=1) + other * jnp.concatenate(
        [sines] * wide, axis=1
    )


def dot_nt(left, right):
    return lax.dot_general(
        left, right, (((1,), (1,)), ((), ())), preferred_element_type=jnp.float32
    )


def dot_nn(left, right):
    return jnp.dot(left, right, preferred_element_type=jnp.float32)


def head_lanes(values, head):
    lanes = lax.broadcasted_iota(jnp.int32, values.shape, 1) // HEAD_DIM
    return jnp.where(lanes == head, values, jnp.zeros_like(values))


def fill_bias(bias_ref, key_segments, query_segments, j, size):
    query_row = query_segments[:, j * size : (j + 1) * size]
    for i in range(j + 1):
        same = key_segments[i * size : (i + 1) * size, :1] == query_row
        if i == j:
            key_at = lax.broadcasted_iota(jnp.int32, (size, size), 0)
            query_at = lax.broadcasted_iota(jnp.int32, (size, size), 1)
            same = same & (key_at <= query_at)
        bias_ref[i] = jnp.where(same, 0.0, MASKED)


def in_order(chunks, near_ref, far_ref, held_ref):
    size = near_ref.shape[0] // 2
    for s in range(CHUNKS):
        source = near_ref if s < 2 else far_ref
        held_ref[pl.ds(pl.multiple_of(chunks[s] * size, size), size), :] = source[
            (s % 2) * size : (s % 2 + 1) * size, :
        ]


def in_pieces(chunks, held_ref, near_ref, far_ref):
    size = near_ref.shape[0] // 2
    for s in range(CHUNKS):
        target = near_ref if s < 2 else far_ref
        target[(s % 2) * size : (s % 2 + 1) * size, :] = held_ref[
            pl.ds(pl.multiple_of(chunks[s] * size, size), size), :
        ].astype(target.dtype)


def attend_kernel(
    chunks, qn, qf, kn, kf, vn, vf, key_segments, query_segments,
    out_near, out_far, lse_ref, q_all, k_all, v_all, vt_ref, ot_ref, out_all, bias_ref,
):
    in_order(chunks, qn, qf, q_all)
    in_order(chunks, kn, kf, k_all)
    in_order(chunks, vn, vf, v_all)
    size = q_all.shape[0] // CHUNKS
    heads = q_all.shape[1] // HEAD_DIM
    lse_ref[...] = jnp.zeros_like(lse_ref)
    for i in range(CHUNKS):
        here = slice(i * size, (i + 1) * size)
        vt_ref[:, here] = v_all[here, :].T
    for j in range(CHUNKS):
        fill_bias(bias_ref, key_segments, query_segments, j, size)
        mine = slice(j * size, (j + 1) * size)

        def one_head(head):
            query = head_lanes(q_all[mine, :], head) * jnp.bfloat16(HEAD_DIM**-0.5)
            features = slice(head * HEAD_DIM, (head + 1) * HEAD_DIM)
            row = slice(head, head + 1)
            scores = [
                dot_nt(k_all[i * size : (i + 1) * size, :], query) + bias_ref[i]
                for i in range(j + 1)
            ]
            top = functools.reduce(
                jnp.maximum, [jnp.max(s, axis=0, keepdims=True) for s in scores]
            )
            expo = [jnp.exp(s - top) for s in scores]
            total = sum(jnp.sum(e, axis=0, keepdims=True) for e in expo)
            mixed = sum(
                dot_nn(vt_ref[features, i * size : (i + 1) * size], expo[i].astype(jnp.bfloat16))
                for i in range(j + 1)
            )
            ot_ref[features, :] = mixed * (1.0 / total)
            lse_ref[row, mine] = top + jnp.log(total)

        for head in range(heads):
            one_head(head)
        out_all[mine, :] = ot_ref[...].T.astype(out_all.dtype)
    in_pieces(chunks, out_all, out_near, out_far)


def attend_back_kernel(
    chunks, qn, qf, kn, kf, vn, vf, don, dof, on, of, lse_ref, key_segments, query_segments,
    cos_near, cos_far, sin_near, sin_far, near_ref, far_ref,
    q_all, k_all, v_all, do_all, o_all, kt_ref, dqt_ref, delta_ref, bias_ref, dq_sum, dk_sum, dv_sum,
):
    for near, far, held in ((qn, qf, q_all), (kn, kf, k_all), (vn, vf, v_all), (don, dof, do_all), (on, of, o_all)):
        in_order(chunks, near, far, held)
    size = q_all.shape[0] // CHUNKS
    heads = q_all.shape[1] // HEAD_DIM
    for i in range(CHUNKS):
        here = slice(i * size, (i + 1) * size)
        kt_ref[:, here] = k_all[here, :].T
    dk_sum[...] = jnp.zeros_like(dk_sum)
    dv_sum[...] = jnp.zeros_like(dv_sum)
    for j in range(CHUNKS):
        fill_bias(bias_ref, key_segments, query_segments, j, size)
        mine = slice(j * size, (j + 1) * size)
        delta_ref[...] = (
            do_all[mine, :].astype(jnp.float32) * o_all[mine, :].astype(jnp.float32)
        ).T

        def one_head(head):
            query = head_lanes(q_all[mine, :], head) * jnp.bfloat16(HEAD_DIM**-0.5)
            upstream = head_lanes(do_all[mine, :], head)
            features = slice(head * HEAD_DIM, (head + 1) * HEAD_DIM)
            row = slice(head, head + 1)
            delta = jnp.sum(delta_ref[features, :], axis=0, keepdims=True)
            lse = lse_ref[row, mine]
            dqt = jnp.zeros((HEAD_DIM, size), jnp.float32)
            for i in range(j + 1):
                here = slice(i * size, (i + 1) * size)
                probs = jnp.exp(dot_nt(k_all[here, :], query) + bias_ref[i] - lse)
                dprobs = dot_nt(v_all[here, :], upstream)
                dscores = (probs * (dprobs - delta)).astype(jnp.bfloat16)
                dv_sum[here, :] += dot_nn(probs.astype(jnp.bfloat16), upstream)
                dk_sum[here, :] += dot_nn(dscores, query)
                dqt += dot_nn(kt_ref[features, here], dscores)
            dqt_ref[features, :] = dqt

        for head in range(heads):
            one_head(head)
        dq_sum[mine, :] = dqt_ref[...].T * HEAD_DIM**-0.5
    width = q_all.shape[1]
    for s in range(CHUNKS):
        target, cosines, sines = (
            (near_ref, cos_near, sin_near) if s < 2 else (far_ref, cos_far, sin_far)
        )
        there = slice((s % 2) * size, (s % 2 + 1) * size)
        here = pl.ds(pl.multiple_of(chunks[s] * size, size), size)
        for n, held in enumerate((dq_sum, dk_sum)):
            target[there, n * width : (n + 1) * width] = rotate(
                held[here, :], cosines[there, :], -sines[there, :]
            ).astype(jnp.bfloat16)
        target[there, 2 * width :] = dv_sum[here, :].astype(jnp.bfloat16)


def halves(tokens, width, kind):
    return [jax.ShapeDtypeStruct((tokens // 2, width), kind)] * 2


def attend_forward(chunks, queries, keys_in, values_in, key_segments, query_segments):
    tokens, width = query_segments.shape[1], queries[0].shape[1]
    size = tokens // CHUNKS
    near, far, lse = pl.pallas_call(
        attend_kernel,
        out_shape=(
            *halves(tokens, width, jnp.bfloat16),
            jax.ShapeDtypeStruct((8, tokens), jnp.float32),
        ),
        in_specs=[SMEM] + [VMEM] * 8,
        out_specs=(VMEM,) * 3,
        scratch_shapes=[pltpu.VMEM((tokens, width), jnp.bfloat16)] * 3
        + [
            pltpu.VMEM((width, tokens), jnp.bfloat16),
            pltpu.VMEM((width, size), jnp.float32),
            pltpu.VMEM((tokens, width), jnp.bfloat16),
            pltpu.VMEM((CHUNKS, size, size), jnp.float32),
        ],
        cost_estimate=pl.CostEstimate(
            flops=4 * tokens * tokens * width,
            bytes_accessed=8 * tokens * width,
            transcendentals=4 * tokens * tokens,
        ),
        compiler_params=grant(14 << 20),
        name="attend_forward",
    )(chunks, *queries, *keys_in, *values_in, key_segments, query_segments)
    return (near, far), lse


def attend_backward(
    chunks, queries, keys_in, values_in, grad_attended, attended, lse, key_segments,
    query_segments, cosines, sines,
):
    tokens, width = query_segments.shape[1], queries[0].shape[1]
    size = tokens // CHUNKS
    return pl.pallas_call(
        attend_back_kernel,
        out_shape=halves(tokens, 3 * width, jnp.bfloat16),
        in_specs=[SMEM] + [VMEM] * 17,
        out_specs=[VMEM] * 2,
        scratch_shapes=[pltpu.VMEM((tokens, width), jnp.bfloat16)] * 5
        + [
            pltpu.VMEM((width, tokens), jnp.bfloat16),
            pltpu.VMEM((width, size), jnp.float32),
            pltpu.VMEM((width, size), jnp.float32),
            pltpu.VMEM((CHUNKS, size, size), jnp.float32),
        ]
        + [pltpu.VMEM((tokens, width), jnp.float32)] * 3,
        cost_estimate=pl.CostEstimate(
            flops=10 * tokens * tokens * width,
            bytes_accessed=16 * tokens * width,
            transcendentals=4 * tokens * tokens,
        ),
        compiler_params=grant(22 << 20),
        name="attend_backward",
    )(
        chunks, *queries, *keys_in, *values_in, *grad_attended, *attended, lse,
        key_segments, query_segments, *cosines, *sines,
    )


def outer_sum(left, right):
    return lax.dot_general(
        left, right, (((0,), (0,)), ((), ())), preferred_element_type=jnp.float32
    )


def grant(moved, scratch=0):
    return pltpu.CompilerParams(vmem_limit_bytes=moved + scratch + (4 << 20))


def call(kernel, name, outs, *args, scratch=(), flops=0, transcendentals=0):
    moved = sum(a.size * a.dtype.itemsize for a in args)
    moved += sum(math.prod(shape) * jnp.dtype(kind).itemsize for shape, kind in outs)
    return pl.pallas_call(
        kernel,
        out_shape=[jax.ShapeDtypeStruct(shape, kind) for shape, kind in outs],
        in_specs=[VMEM] * len(args),
        out_specs=[VMEM] * len(outs),
        scratch_shapes=scratch,
        cost_estimate=pl.CostEstimate(
            flops=flops, bytes_accessed=moved, transcendentals=transcendentals
        ),
        compiler_params=grant(moved),
        name=name,
    )(*args)


def qkv_kernel(first, second, weight, cosines, sines, q_ref, k_ref, v_ref):
    size, width = first.shape[0], q_ref.shape[1]
    for p, rows in enumerate((first, second)):
        here = slice(p * size, (p + 1) * size)
        for n, target in enumerate((q_ref, k_ref, v_ref)):
            values = dot_nn(rows[...], weight[:, n * width : (n + 1) * width])
            if n < 2:
                values = rotate(values, cosines[here, :], sines[here, :])
            target[here, :] = values.astype(jnp.bfloat16)


def qkv_rows(pieces, weight, cosines, sines):
    rows, width = 2 * pieces[0].shape[0], weight.shape[1] // 3
    return call(
        qkv_kernel,
        "qkv_rows",
        [((rows, width), jnp.bfloat16)] * 3,
        *pieces,
        weight,
        cosines,
        sines,
        flops=2 * rows * weight.size,
    )


TILE = 256


def tiles(total, body):
    @pl.loop(0, total // TILE)
    def _(n):
        body(pl.ds(pl.multiple_of(n * TILE, TILE), TILE))


def back_kernel(rows, weight, first, second):
    size = first.shape[0]

    def tile(columns):
        values = dot_nt(rows[...], weight[columns, :])
        first[:, columns] = values[:size]
        second[:, columns] = values[size:].astype(jnp.bfloat16)

    tiles(weight.shape[0], tile)


def project_back(rows, weight):
    size = rows.shape[0] // 2
    return call(
        back_kernel,
        "project_back",
        [((size, weight.shape[0]), jnp.float32), ((size, weight.shape[0]), jnp.bfloat16)],
        rows,
        weight,
        flops=2 * rows.shape[0] * weight.size,
    )


ROOT = math.sqrt(2.0 / math.pi)
CUBE = 0.044715


def up_kernel(first, second, weight, act_ref, slope_ref):
    size = first.shape[0]

    def tile(columns):
        for p, rows in enumerate((first, second)):
            here = slice(p * size, (p + 1) * size)
            up = dot_nn(rows[...], weight[:, columns])
            square = up * up
            bent = jnp.tanh(up * (ROOT + (ROOT * CUBE) * square))
            half = 0.5 + 0.5 * bent
            act_ref[here, columns] = (up * half).astype(jnp.bfloat16)
            slope = half + (half - half * bent) * up * (ROOT + (3.0 * ROOT * CUBE) * square)
            slope_ref[here, columns] = slope.astype(jnp.bfloat16)

    tiles(weight.shape[1], tile)


def up_rows(pieces, weight):
    shape = (2 * pieces[0].shape[0], weight.shape[1])
    return call(
        up_kernel,
        "up_rows",
        [(shape, jnp.bfloat16)] * 2,
        *pieces,
        weight,
        flops=2 * shape[0] * weight.size,
        transcendentals=shape[0] * shape[1],
    )


def up_back_kernel(first, second, weight, slope_ref, out_ref):
    size = first.shape[0]

    def tile(columns):
        for p, rows in enumerate((first, second)):
            here = slice(p * size, (p + 1) * size)
            grad = dot_nn(rows[...], weight[:, columns])
            grad = grad * slope_ref[here, columns].astype(jnp.float32)
            out_ref[here, columns] = grad.astype(jnp.bfloat16)

    tiles(weight.shape[1], tile)


def up_back(pieces, weight, slope):
    return call(
        up_back_kernel,
        "up_back",
        [(slope.shape, jnp.bfloat16)],
        *pieces,
        weight,
        slope,
        flops=2 * slope.shape[0] * weight.size,
    )[0]


def plain_kernel(first, second, weight, out_ref):
    size = first.shape[0]
    for p, rows in enumerate((first, second)):
        out_ref[p * size : (p + 1) * size, :] = dot_nn(rows[...], weight[...]).astype(jnp.bfloat16)


def project(pieces, weight):
    shape = (2 * pieces[0].shape[0], weight.shape[1])
    return call(
        plain_kernel,
        "project",
        [(shape, jnp.bfloat16)],
        *pieces,
        weight,
        flops=2 * shape[0] * weight.size,
    )[0]


STEP = 32


def row_steps(total, body):
    @pl.loop(0, total // STEP)
    def _(n):
        body(pl.ds(pl.multiple_of(n * STEP, STEP), STEP))


def normed(values):
    centred = values - jnp.mean(values, axis=-1, keepdims=True)
    variance = jnp.mean(centred * centred, axis=-1, keepdims=True)
    inv_std = lax.rsqrt(variance + EPSILON)
    return centred * inv_std, inv_std


def norm_back(upstream, hat, inv_std, gain):
    scaled = upstream * gain
    first_mean = jnp.mean(scaled, axis=-1, keepdims=True)
    cross_mean = jnp.mean(scaled * hat, axis=-1, keepdims=True)
    return inv_std * (scaled - first_mean - hat * cross_mean)


def add_rows(sum_ref, index, values):
    sum_ref[index] += functools.reduce(
        jnp.add, [values[i : i + 8, :] for i in range(0, values.shape[0], 8)]
    )


def whole(own, beside, far, rows):
    return own[rows, :] + beside[rows, :].astype(jnp.float32) + far[rows, :].astype(jnp.float32)


def start_kernel(residual, params, valid, a_ref, sums, held):
    held[...] = jnp.zeros_like(held)

    def step(rows):
        values = residual[rows, :].astype(jnp.float32)
        hat, _ = normed(values)
        a_ref[rows, :] = (hat * params[0:1, :] + params[4:5, :]).astype(jnp.bfloat16)
        add_rows(held, 0, values * values * valid[rows, :1])

    row_steps(residual.shape[0], step)
    sums[...] = jnp.sum(held[...], axis=1)


def middle_kernel(own, beside, far, residual, params, valid, raw_ref, h_ref, b_ref, sums, held):
    held[...] = jnp.zeros_like(held)

    def step(rows):
        raw = whole(own, beside, far, rows)
        raw_ref[rows, :] = raw
        hat, _ = normed(raw)
        hidden = residual[rows, :].astype(jnp.float32) + (hat * params[1:2, :] + params[5:6, :])
        h_ref[rows, :] = hidden
        hat, _ = normed(hidden)
        b_ref[rows, :] = (hat * params[2:3, :] + params[6:7, :]).astype(jnp.bfloat16)
        add_rows(held, 0, raw * raw * valid[rows, :1])

    row_steps(residual.shape[0], step)
    sums[...] = jnp.sum(held[...], axis=1)


def top_kernel(
    own, beside, far, hidden, cotangent, params, valid, out_ref, grad_ref, sums, held
):
    held[...] = jnp.zeros_like(held)

    def step(rows):
        raw = whole(own, beside, far, rows)
        hat, inv_std = normed(raw)
        out = hidden[rows, :] + (hat * params[3:4, :] + params[7:8, :])
        out_ref[rows, :] = out.astype(jnp.bfloat16)
        upstream = cotangent[rows, :].astype(jnp.float32) * valid[rows, :1]
        grad = norm_back(upstream, hat, inv_std, params[3:4, :])
        grad_ref[rows, :] = grad.astype(jnp.bfloat16)
        add_rows(held, 0, raw * raw * valid[rows, :1])
        add_rows(held, 1, upstream * hat)
        add_rows(held, 2, upstream)

    row_steps(hidden.shape[0], step)
    sums[...] = jnp.sum(held[...], axis=1)


def middle_back_kernel(
    own, beside, far, hidden, raw_attn, cotangent, params, valid, dh_ref, grad_ref, sums, held
):
    held[...] = jnp.zeros_like(held)

    def step(rows):
        grad_b = whole(own, beside, far, rows)
        hat, inv_std = normed(hidden[rows, :])
        add_rows(held, 0, grad_b * hat)
        add_rows(held, 1, grad_b)
        upstream = cotangent[rows, :].astype(jnp.float32) * valid[rows, :1]
        grad_h = upstream + norm_back(grad_b, hat, inv_std, params[2:3, :])
        dh_ref[rows, :] = grad_h
        hat, inv_std = normed(raw_attn[rows, :])
        add_rows(held, 2, grad_h * hat)
        add_rows(held, 3, grad_h)
        grad = norm_back(grad_h, hat, inv_std, params[1:2, :])
        grad_ref[rows, :] = grad.astype(jnp.bfloat16)

    row_steps(hidden.shape[0], step)
    sums[...] = jnp.sum(held[...], axis=1)


def end_kernel(own, beside, far, residual, grad_h, params, out_ref, sums, held):
    held[...] = jnp.zeros_like(held)

    def step(rows):
        grad_a = whole(own, beside, far, rows)
        hat, inv_std = normed(residual[rows, :].astype(jnp.float32))
        add_rows(held, 0, grad_a * hat)
        add_rows(held, 1, grad_a)
        grad = grad_h[rows, :] + norm_back(grad_a, hat, inv_std, params[0:1, :])
        out_ref[rows, :] = grad.astype(jnp.bfloat16)

    row_steps(residual.shape[0], step)
    sums[...] = jnp.sum(held[...], axis=1)


def on_rows(kernel, name, kinds, count, *args):
    shape = args[0].shape
    return call(
        kernel,
        name,
        [(shape, kind) for kind in kinds] + [((count, shape[1]), jnp.float32)],
        *args,
        scratch=[pltpu.VMEM((count, 8, shape[1]), jnp.float32)],
        flops=40 * shape[0] * shape[1],
    )


def per_device(
    residual_in,
    segments,
    positions,
    query_weight,
    key_weight,
    value_weight,
    out_weight,
    up_weight,
    down_weight,
    norm_gains,
    norm_biases,
    cotangent,
):
    place = Place()
    local_rows = residual_in.shape[0]
    group_rows = segments.shape[0]
    grad_scale = 1.0 / math.sqrt(group_rows * lax.axis_size("dp"))
    bf16, f32 = jnp.bfloat16, jnp.float32

    qkv_block = jnp.concatenate([query_weight, key_weight, value_weight], axis=1)
    qkv_other = exchange(qkv_block, Z_HI)
    residual = move_tokens(residual_in)
    numbers = jnp.stack([segments, positions])
    numbers = jnp.where(place.at_home, numbers, exchange(numbers, CORE))
    query_segments = numbers[:1]
    key_segments = jnp.broadcast_to(numbers[0][:, None], (group_rows, 128))
    numbers = numbers.reshape(2, 4, local_rows)
    numbers = jnp.stack([pick(numbers, 1, place.chunk ^ p) for p in PIECES], axis=1)
    chunks = jnp.stack([place.chunk ^ p for p in PIECES]).astype(jnp.int32)
    valid = (numbers[0, 0] >= 0).astype(f32)[:, None]
    valid_count = jnp.sum(valid)
    valid = jnp.broadcast_to(valid, (local_rows, 128))
    cosines, sines = rotary_tables(numbers[1].reshape(-1))
    cosines, sines = jnp.split(cosines, 2), jnp.split(sines, 2)

    params = jnp.concatenate([norm_gains, norm_biases])
    width = params.shape[1]
    at = (place.dp * lax.axis_size("tensor") + place.tensor) * width
    params = lax.dynamic_update_slice(jnp.zeros((params.shape[0], D), f32), params, (0, at))
    params = sum_everywhere(params)

    (qkv_full,) = gather_weight(qkv_block, qkv_other, place, (qkv_block.shape[1],))
    later_block = jnp.concatenate([out_weight, up_weight], axis=1)
    later_block = after(later_block, (qkv_other, residual))
    later_other = exchange(later_block, Z_HI)
    out_full, up_full = gather_weight(
        later_block, later_other, place, (out_weight.shape[1], up_weight.shape[1])
    )
    down_block = after(down_weight, later_other)
    down_other = exchange(down_block, Z_HI)
    (down_full,) = gather_weight(down_block, down_other, place, (down_weight.shape[1],))
    cotangent_rows = move_tokens(after(cotangent, down_other))

    attn_in, input_sums = on_rows(
        start_kernel, "start", [bf16], 1, residual, params, valid
    )
    attn_rows = gather_rows(attn_in)
    queries, keys, values = zip(
        *[
            qkv_rows(rows, qkv_full, cos_rows, sin_rows)
            for rows, cos_rows, sin_rows in zip(attn_rows, cosines, sines)
        ]
    )
    attended, log_totals = attend_forward(
        chunks, queries, keys, values, key_segments, query_segments
    )
    raw_attn, hidden, mlp_in, attn_sums = on_rows(
        middle_kernel,
        "middle",
        [f32, f32, bf16],
        1,
        *sum_rows(*[project_back(rows, out_full) for rows in attended]),
        residual,
        params,
        valid,
    )
    mlp_rows = gather_rows(mlp_in)
    activated, slopes = zip(*[up_rows(rows, up_full) for rows in mlp_rows])
    layer_out, grad_raw_mlp, top_sums = on_rows(
        top_kernel,
        "top",
        [bf16, bf16],
        3,
        *sum_rows(*[project_back(rows, down_full) for rows in activated]),
        hidden,
        cotangent_rows,
        params,
        valid,
    )
    layer_out = move_tokens(layer_out)
    grad_mlp_rows = gather_rows(grad_raw_mlp)
    grad_up = [up_back(rows, down_full, slope) for rows, slope in zip(grad_mlp_rows, slopes)]
    grad_b = sum_rows(*[project_back(rows, up_full) for rows in grad_up])
    grad_up_weight = reduce_weight(sum(mlp_rows, ()), grad_up, place)
    grad_down_weight = reduce_weight(sum(grad_mlp_rows, ()), activated, place)
    grad_hidden, grad_raw_attn, middle_sums = on_rows(
        middle_back_kernel,
        "middle_back",
        [f32, bf16],
        4,
        *grad_b,
        hidden,
        raw_attn,
        cotangent_rows,
        params,
        valid,
    )
    grad_attn_rows = gather_rows(grad_raw_attn)
    grad_attended = [project(rows, out_full) for rows in grad_attn_rows]
    grad_out_weight = reduce_weight(sum(grad_attn_rows, ()), attended, place)
    grad_qkv = attend_backward(
        chunks,
        queries,
        keys,
        values,
        grad_attended,
        attended,
        log_totals,
        key_segments,
        query_segments,
        cosines,
        sines,
    )
    grad_a = sum_rows(*[project_back(rows, qkv_full) for rows in grad_qkv])
    grad_qkv_weight = reduce_weight(sum(attn_rows, ()), grad_qkv, place)
    grad_input, end_sums = on_rows(
        end_kernel, "end", [bf16], 2, *grad_a, residual, grad_hidden, params
    )
    grad_input = move_tokens(grad_input)
    totals = jnp.concatenate(
        [
            end_sums,
            middle_sums,
            top_sums,
            input_sums,
            attn_sums,
            jnp.pad(valid_count[None, None], ((0, 0), (0, D - 1))),
        ]
    )
    totals = sum_everywhere(totals)
    mine = lax.dynamic_slice(totals, (0, at), (totals.shape[0], width)) * grad_scale
    gain_grads = jnp.stack([mine[0], mine[4], mine[2], mine[7]])
    bias_grads = jnp.stack([mine[1], mine[5], mine[3], mine[8]])
    squares = jnp.sum(totals, axis=1)
    rms_values = jnp.sqrt(
        jnp.stack([squares[9], squares[10], squares[6]]) / (squares[11] * D)
    )
    return (
        layer_out,
        grad_input,
        *jnp.split(grad_qkv_weight * grad_scale, 3, axis=1),
        grad_out_weight * grad_scale,
        grad_up_weight * grad_scale,
        grad_down_weight * grad_scale,
        gain_grads,
        bias_grads,
        rms_values,
    )


def solution(mesh):
    in_specs = (
        P(("dp", "tensor"), None),
        P("dp"),
        P("dp"),
        P("dp", "tensor"),
        P("dp", "tensor"),
        P("dp", "tensor"),
        P("dp", "tensor"),
        P("dp", "tensor"),
        P("dp", "tensor"),
        P(None, ("dp", "tensor")),
        P(None, ("dp", "tensor")),
        P(("dp", "tensor"), None),
    )
    out_specs = (
        P(("dp", "tensor"), None),
        P(("dp", "tensor"), None),
        P("dp", "tensor"),
        P("dp", "tensor"),
        P("dp", "tensor"),
        P("dp", "tensor"),
        P("dp", "tensor"),
        P("dp", "tensor"),
        P(None, ("dp", "tensor")),
        P(None, ("dp", "tensor")),
        P(),
    )
    return jax.shard_map(
        per_device, mesh=mesh, in_specs=in_specs, out_specs=out_specs, check_vma=False
    )
```
